32 devices in a mesh: energy: 16 (over z, y, x), space: 2 (over core).
Axes of the slice: x: 2, y: 2, z: 4, core: 2. Of those that a mesh axis runs over, the one named last changes fastest.
Arguments:
- green0: bfloat16 [128, 2, 2, 192, 192], P('energy', 'space'), may hold values from -1.5 to 1
- coupling: bfloat16 [2, 192, 192], P('space'), may hold values from -0.375 to 0.375
- pattern: int32 [2, 4, 4], P('space'), may hold values 0 or 1
- broaden: bfloat16 [128, 2, 192, 192], P('energy', 'space'), may hold values from -0.5 to 1.5
- screened: float32 [128, 2, 192, 384], P(None, 'space', 'energy'), may hold values from -6 to 6
- order: int32 [192], replicated, may hold values from 0 to 191, each once
Outputs:
- sigma: float32 [128, 2, 192, 384], P('energy', 'space')
The draws below stay inside these ranges and needn't reach their ends.
All inputs are finite; a program needn't handle non-finite values. No bound on the sum of `pattern` on one device may be relied on, other than what follows from the above.
Results may differ from the reference program's by a relative error of at most 0.0059.
Values may be sent and summed in bfloat16 or wider, within the bound.
A program may use at most 128 MiB of HBM per device.

```python
import math
import jax
import jax.numpy as jnp
from jax import lax

BS = 192
TB = 4
NE = 128
NB = 2


def draw_green0(key, part):
    key_list = jax.random.split(key, 3)
    full_shape = (NE, NB, 2, BS, BS)
    rough_part = jnp.clip(jax.random.normal(key_list[0], full_shape, jnp.float32), -4.0, 4.0)
    symmetric = (rough_part + jnp.swapaxes(rough_part, -1, -2)) * (0.3 / math.sqrt(2.0 * BS))
    diag_real = jax.random.uniform(key_list[1], (NE, NB, 1, BS), jnp.float32, -1.0, 1.0)
    diag_imag = jax.random.uniform(key_list[2], (NE, NB, 1, BS), jnp.float32, -1.5, -0.4)
    diag_values = jnp.concatenate([diag_real, diag_imag], axis=2)
    diagonal_ones = jnp.eye(BS, dtype=jnp.float32)
    return (symmetric * (1.0 - diagonal_ones) + diag_values[..., None] * diagonal_ones).astype(jnp.bfloat16)


def draw_broaden(key, part):
    key_list = jax.random.split(key, 2)
    full_shape = (NE, NB, BS, BS)
    rough_part = jnp.clip(jax.random.normal(key_list[0], full_shape, jnp.float32), -4.0, 4.0)
    symmetric = (rough_part + jnp.swapaxes(rough_part, -1, -2)) * (0.3 / math.sqrt(2.0 * BS))
    diag_values = jax.random.uniform(key_list[1], (NE, NB, BS), jnp.float32, 0.2, 1.5)
    diagonal_ones = jnp.eye(BS, dtype=jnp.float32)
    return (symmetric * (1.0 - diagonal_ones) + diag_values[..., None] * diagonal_ones).astype(jnp.bfloat16)


def plant(drawn, own_key, least, high):
    shape = drawn.shape
    spot = [jax.random.randint(jax.random.fold_in(own_key, axis), (), 0, shape[axis]) for axis in range(len(shape))]
    drawn = drawn.at[tuple(spot)].set(least)
    longest = shape.index(max(shape))
    spot[longest] = (spot[longest] + 1) % shape[longest]
    return drawn.at[tuple(spot)].set(high)


def levels(own_key, dims, cuts, smallest, high):
    gain, own = 1.0, jax.random.fold_in(own_key, 6)
    for dim, blocks in cuts:
        heights = jnp.exp(jax.random.uniform(jax.random.fold_in(own, dim), (blocks,), jnp.float32, smallest / len(cuts), high / len(cuts)))
        gain = gain * jnp.repeat(heights, dims[dim] // blocks).reshape([-1 if axis == dim else 1 for axis in range(len(dims))])
    return gain


def normal_values(stream_key, shape, width, reach, cuts=(), kind=jnp.bfloat16):
    result = width * jax.random.normal(stream_key, shape, jnp.float32)
    if cuts:
        result = result * levels(stream_key, shape, cuts, -0.22, 0.18)
    return jnp.clip(result, -reach, reach).astype(kind)


def setup_inputs(seed: int = 0) -> dict:
    streams_of = jax.random.split(jax.random.key(seed), 7)
    return {
        "green0": draw_green0(jax.random.fold_in(streams_of[6], 71), 0),
        "coupling": normal_values(streams_of[1], (NB, BS, BS), (5 * BS // 4) ** -0.5, 0.375, ((0, 2),)),
        "pattern": plant((jax.random.randint(streams_of[2], (NB, TB, TB), 0, 4) < 3).astype(jnp.int32), jax.random.fold_in(streams_of[2], 1), 0, 1),
        "broaden": draw_broaden(jax.random.fold_in(streams_of[6], 71), 0),
        "screened": normal_values(streams_of[4], (NE, NB, BS, 2 * BS), 1.0, 6.0, ((1, 2), (2, 16)), jnp.float32),
        "order": jax.random.permutation(streams_of[5], BS).astype(jnp.int32),
    }


def to_half(values):
    return values.astype(jnp.bfloat16)

def flip_last(values):
    return jnp.swapaxes(values, -1, -2)

def complex_product(left_op, right_op):
    left_op = left_op.astype(jnp.float32)
    right_op = right_op.astype(jnp.float32)

    def matmul(first_op, second):
        return jnp.einsum('...ij,...jk->...ik', first_op, second)
    real_part = matmul(left_op[..., 0, :, :], right_op[..., 0, :, :]) - matmul(left_op[..., 1, :, :], right_op[..., 1, :, :])
    imag_part = matmul(left_op[..., 0, :, :], right_op[..., 1, :, :]) + matmul(left_op[..., 1, :, :], right_op[..., 0, :, :])
    return jnp.stack([real_part, imag_part], axis=-3)

def reference(green0, coupling, pattern, broaden, screened, order):
    tile_size = BS // TB
    spread = jnp.repeat(jnp.repeat(pattern, tile_size, axis=1), tile_size, axis=2)
    couple = coupling * spread.astype(jnp.bfloat16)
    couple_f = couple.astype(jnp.float32)

    def one_energy(items):
        green_cell, gamma_cell = items
        green_f = green_cell.astype(jnp.float32)
        factor = to_half(jnp.einsum('bcij,bjk->bcik', green_f, couple_f))
        added_term = to_half(jnp.einsum('bcij,bjk->bcik', flip_last(factor).astype(jnp.float32), couple_f))

        def left_step(carried, pieces):
            green_b, factor_b = pieces
            left_b = green_b.astype(jnp.float32) + complex_product(to_half(complex_product(factor_b, carried)), flip_last(factor_b))
            return (to_half(left_b), left_b)
        unused, left_part = lax.scan(left_step, green_cell[0], (green_cell, factor))

        def right_step(passed, pieces):
            green_b, factor_b, added_b = pieces
            right_b = green_b.astype(jnp.float32) + complex_product(to_half(complex_product(green_b, passed)), green_b)
            moved = to_half(complex_product(flip_last(factor_b), passed))
            passed_next = to_half(complex_product(moved, factor_b) + added_b.astype(jnp.float32))
            return (passed_next, right_b)
        unused, right_part = lax.scan(right_step, jnp.zeros_like(green_cell[0]), (green_cell, factor, added_term), reverse=True)
        full_green = to_half(left_part + right_part - green_f).astype(jnp.float32)
        weighted = to_half(jnp.einsum('bcij,bjk->bcik', full_green, gamma_cell.astype(jnp.float32))).astype(jnp.float32)

        def outer_product(first_op, second):
            return jnp.einsum('bij,bkj->bik', first_op, second)
        real_part = outer_product(weighted[:, 0], full_green[:, 1]) - outer_product(weighted[:, 1], full_green[:, 0])
        imag_part = outer_product(weighted[:, 0], full_green[:, 0]) + outer_product(weighted[:, 1], full_green[:, 1])
        return jnp.concatenate([real_part, imag_part], axis=-1)
    lesser = lax.map(one_energy, (green0, broaden))
    slotted = jnp.take(lesser, order, axis=2)

    def convolve(items):
        values, kernel = items
        value_c = values[..., :BS] + 1j * values[..., BS:]
        kernel_c = kernel[..., :BS] + 1j * kernel[..., BS:]
        mixed = jnp.fft.ifft(jnp.fft.fft(value_c, axis=0) * jnp.fft.fft(kernel_c, axis=0), axis=0) * (1j / math.sqrt(NE))
        return jnp.concatenate([jnp.real(mixed), jnp.imag(mixed)], axis=-1)
    sigma_slot = lax.map(convolve, (jnp.moveaxis(slotted, 1, 0), jnp.moveaxis(screened, 1, 0)))
    sigma_slot = jnp.moveaxis(sigma_slot, 0, 1)
    sigma_rows = jnp.zeros_like(sigma_slot).at[:, :, order, :].set(sigma_slot)
    return sigma_rows.astype(jnp.float32)
```

```python
import functools
import math

import jax
import jax.numpy as jnp
import numpy as np
from jax import lax
from jax.experimental import pallas as pl
from jax.experimental.pallas import tpu as pltpu
from jax.sharding import PartitionSpec as P

F32 = jnp.float32
BF16 = jnp.bfloat16
PLAIN = ((1,), (0,))
LAST = ((1,), (1,))
FIRST = ((0,), (0,))


def dot(a, b, dims=PLAIN):
    return lax.dot_general(a, b, (dims, ((), ())), preferred_element_type=F32)


def complex_dot(left, right_re, right_im, dims=PLAIN):
    rows = left.shape[0] // 2
    with_re = dot(left, right_re, dims)
    with_im = dot(left, right_im, dims)
    return (with_re[:rows] - with_im[rows:], with_im[:rows] + with_re[rows:])


def stack(pair):
    return jnp.concatenate(pair, axis=0)


def times_i(values):
    half = values.shape[1] // 2
    return jnp.concatenate([-values[:, half:], values[:, :half]], axis=1)


def transform(table, upper, lower):
    both = dot(table, jnp.concatenate([upper, lower], axis=0).astype(BF16))
    points = upper.shape[0]
    return both[:points] + both[points:]


def fused_kernel(
    owners,
    pack,
    scale,
    pattern_ref,
    coupling_ref,
    green_ref,
    gamma_ref,
    order_ref,
    sort_ref,
    turn_ref,
    table_ref,
    unmix_ref,
    screened_ref,
    out_ref,
    coupling_s,
    couple_s,
    turned_s,
    green_s,
    gamma_s,
    order_s,
    sort_s,
    turn_s,
    table_s,
    unmix_s,
    screened_s,
    mult_s,
    other_s,
    base_s,
    send_s,
    map_s,
    pick_s,
    place_s,
    mixed_s,
    got_s,
    spectrum_s,
    sigma_s,
    back_s,
    slots_s,
    result_s,
    load_sem,
    green_sem,
    out_sem,
    map_sent,
    map_landed,
    early_sent,
    early_landed,
    late_sent,
    late_landed,
    back_sent,
    back_landed,
    own_early,
    own_late,
    own_back,
):
    me = lax.axis_index("energy")
    cell = lax.axis_index("space")
    here, both, size = green_s.shape
    rows = both // 2
    width = 2 * size
    share = size // owners
    quads = share // pack
    many = 8 // pack
    batches = here // many
    points = owners * here
    early = max(quads - 1, 1)

    def load(n, source, target):
        return pltpu.make_async_copy(source, target, load_sem.at[n])

    def load_green(b):
        at = pl.ds(b * many, many)
        return pltpu.make_async_copy(green_ref.at[at], green_s.at[at], green_sem.at[b])

    loads = [
        load(n, source, target)
        for n, (source, target) in enumerate(
            (
                (coupling_ref, coupling_s),
                (order_ref, order_s),
                (sort_ref, sort_s),
                (gamma_ref, gamma_s),
                (table_ref, table_s),
                (screened_ref, screened_s),
                (turn_ref, turn_s),
                (unmix_ref, unmix_s),
            )
        )
    ]
    coupling_load, order_load, sort_load, gamma_load, table_load, screened_load, turn_load, unmix_load = loads

    def peer_of(k):
        return lax.rem(me + k, owners)

    def remote(source, target, sent, landed, device):
        return pltpu.make_async_remote_copy(
            src_ref=source,
            dst_ref=target,
            send_sem=sent,
            recv_sem=landed,
            device_id=device,
            device_id_type=pl.DeviceIdType.MESH,
        )

    def share_map(b):
        at = pl.ds(b * many, many)
        return remote(send_s.at[at], map_s.at[at], map_sent.at[b], map_landed.at[b], {"space": 1 - cell})

    def away_early(b, k):
        peer = peer_of(k)
        columns = pl.ds(0, early * width)
        return remote(
            mixed_s.at[peer, b, :, columns],
            got_s.at[me, b, :, columns],
            early_sent.at[b, k - 1],
            early_landed.at[b, k - 1],
            {"energy": peer},
        )

    def away_late(k):
        peer = peer_of(k)
        columns = pl.ds(early * width, (quads - early) * width)
        return remote(
            mixed_s.at[peer, :, :, columns],
            got_s.at[me, :, :, columns],
            late_sent.at[k - 1],
            late_landed.at[k - 1],
            {"energy": peer},
        )

    def back(q, k):
        peer = peer_of(k)
        columns = pl.ds(q * pack * width, pack * width)
        return remote(
            sigma_s.at[peer, :, columns],
            back_s.at[me, :, columns],
            back_sent.at[q, k - 1],
            back_landed.at[q, k - 1],
            {"energy": peer},
        )

    def keep_early(b):
        columns = pl.ds(0, early * width)
        return pltpu.make_async_copy(
            mixed_s.at[me, b, :, columns], got_s.at[me, b, :, columns], own_early.at[b]
        )

    def keep_late():
        columns = pl.ds(early * width, (quads - early) * width)
        return pltpu.make_async_copy(
            mixed_s.at[me, :, :, columns], got_s.at[me, :, :, columns], own_late.at[0]
        )

    def keep_back(q):
        columns = pl.ds(q * pack * width, pack * width)
        return pltpu.make_async_copy(
            sigma_s.at[me, :, columns], back_s.at[me, :, columns], own_back.at[q]
        )

    def for_peers(action):
        lax.fori_loop(1, owners, lambda k, c: (action(k), c)[1], 0)

    barrier = pltpu.get_barrier_semaphore()

    def greet(device):
        pl.semaphore_signal(barrier, inc=1, device_id=device, device_id_type=pl.DeviceIdType.MESH)

    coupling_load.start()
    load_green(0).start()
    for_peers(lambda k: greet({"energy": peer_of(k)}))
    greet({"space": 1 - cell})
    for b in range(1, batches):
        load_green(b).start()
    for each in loads[1:]:
        each.start()

    tiles = pattern_ref.shape[0]
    tile_size = size // tiles
    coupling_load.wait()
    lane = lax.broadcasted_iota(jnp.int32, (tile_size, size), 1)
    for i in range(tiles):
        keep = jnp.zeros((tile_size, size), F32)
        for j in range(tiles):
            inside = (lane >= j * tile_size) & (lane < (j + 1) * tile_size)
            keep = jnp.where(inside, pattern_ref[i, j].astype(F32), keep)
        at = slice(i * tile_size, (i + 1) * tile_size)
        couple_s[at, :] = (coupling_s[at, :].astype(F32) * keep).astype(BF16)

    @pl.when(cell == 1)
    def _():
        turned_s[...] = jnp.transpose(couple_s[...].astype(F32)).astype(BF16)

    def born(b):
        load_green(b).wait()
        batch = [b * many + i for i in range(many)]

        @pl.when(cell == 0)
        def _():
            couple = couple_s[...]
            green = [green_s[e] for e in batch]
            factor = [dot(g, couple).astype(BF16) for g in green]
            moved = [
                stack(complex_dot(f, g[:rows], g[rows:])).astype(BF16) for f, g in zip(factor, green)
            ]
            for e, f, g, m in zip(batch, factor, green, moved):
                base = g.astype(F32) + stack(complex_dot(m, f[:rows], f[rows:], LAST))
                base_s[e] = base
                send_s[e] = base.astype(BF16)
                mult_s[e] = g
                other_s[e] = g

        @pl.when(cell == 1)
        def _():
            couple = couple_s[...]
            turned = turned_s[...]
            green = [green_s[e] for e in batch]
            flipped = [
                stack((dot(turned, g[:rows], LAST), dot(turned, g[rows:], LAST))).astype(BF16)
                for g in green
            ]
            for e, f in zip(batch, flipped):
                send_s[e] = dot(f, couple).astype(BF16)
                other_s[e] = f
            for e, g in zip(batch, green):
                mult_s[e] = dot(g, couple).astype(BF16)
                base_s[e] = g.astype(F32)

    def lesser(b):
        batch = [b * many + i for i in range(many)]
        mult = [mult_s[e] for e in batch]
        other = [other_s[e] for e in batch]
        moved = [
            stack(complex_dot(m, map_s[e, :rows], map_s[e, rows:])).astype(BF16)
            for e, m in zip(batch, mult)
        ]
        full = [
            (base_s[e] + stack(complex_dot(m, o[:rows], o[rows:]))).astype(BF16)
            for e, m, o in zip(batch, moved, other)
        ]
        weighted = [dot(f, gamma_s[e]).astype(BF16) for e, f in zip(batch, full)]
        found = [
            (
                dot(w[:rows], stack((f[rows:], f[:rows])), LAST)
                + dot(w[rows:], stack((-f[:rows], f[rows:])), LAST)
            ).astype(BF16)
            for w, f in zip(weighted, full)
        ]
        block = 8 * owners
        for q in range(quads):
            at = slice(q * block, (q + 1) * block)
            mixed = sum(dot(pick_s[i, at], found[i]) for i in range(many))
            mixed_s[:, b, :, q * width : (q + 1) * width] = mixed.reshape(owners, 8, width).astype(BF16)

    born(0)
    pl.semaphore_wait(barrier, owners)
    share_map(0).start()
    if batches > 1:
        born(1)
        share_map(1).start()
    order_load.wait()
    sort_load.wait()
    ids = lax.broadcasted_iota(jnp.int32, (size, size), 0)
    place = jnp.where(ids == order_s[...], 1.0, 0.0).astype(BF16)
    for i in range(many):
        pick_s[i] = dot(sort_s[i], place, LAST).astype(BF16)
    gamma_load.wait()

    for b in range(batches):
        share_map(b).wait_recv()
        lesser(b)
        for_peers(lambda k: away_early(b, k).start())
        keep_early(b).start()
        if b + 2 < batches:
            born(b + 2)
            share_map(b + 2).start()
    if quads > early:
        for_peers(lambda k: away_late(k).start())
        keep_late().start()
    turn_load.wait()
    place_s[...] = dot(place, turn_s[...]).astype(BF16)
    table_load.wait()
    screened_load.wait()
    unmix_load.wait()
    table = table_s[...]
    pieces = width // 128
    for r in range(share):
        values = jnp.concatenate(
            [
                screened_s[pl.ds(r * pieces + c, points, stride=share * pieces), :]
                for c in range(pieces)
            ],
            axis=1,
        )
        spectrum_s[:, r * width : (r + 1) * width] = transform(table, values, times_i(values)) * scale

    half = width // 2
    row_ids = lax.broadcasted_iota(jnp.int32, (points, points * pack), 0)
    column_ids = lax.broadcasted_iota(jnp.int32, (points, points * pack), 1)
    for q in range(quads):
        if q == 0:
            lax.fori_loop(
                0, batches, lambda b, c: (for_peers(lambda k: away_early(b, k).wait_recv()), c)[1], 0
            )
            for b in range(batches):
                keep_early(b).wait()
        if q == early:
            for_peers(lambda k: away_late(k).wait_recv())
            keep_late().wait()
        packed = got_s[:, :, :, q * width : (q + 1) * width].astype(F32)
        packed = packed.reshape(points * pack, width).astype(BF16)
        for r in range(pack):
            if pack == 1:
                values = packed.astype(F32)
            else:
                chosen = jnp.where(column_ids == row_ids * pack + r, 1.0, 0.0).astype(BF16)
                values = dot(chosen, packed)
            at = slice((q * pack + r) * width, (q * pack + r + 1) * width)
            kernel = spectrum_s[:, at]
            spectrum = transform(table, values, times_i(values))
            kernel_re = jnp.concatenate([kernel[:, :half], kernel[:, :half]], axis=1)
            kernel_im = jnp.concatenate([kernel[:, half:], kernel[:, half:]], axis=1)
            product = spectrum * kernel_re + times_i(spectrum) * kernel_im
            found = transform(table, times_i(product), product)
            sigma_s[:, :, at] = found.reshape(owners, here, width).astype(BF16)
        for_peers(lambda k: back(q, k).start())
        keep_back(q).start()

    unmix = unmix_s[...]
    for q in range(quads):
        for_peers(lambda k: back(q, k).wait_recv())
        keep_back(q).wait()
        for r in range(q * pack, (q + 1) * pack):
            values = back_s[:, :, r * width : (r + 1) * width].astype(F32)
            values = values.reshape(points, width).astype(BF16)
            slots_s[r] = dot(unmix, values).astype(BF16)
    outs = []
    for e in range(here):
        at = slice(e * owners, (e + 1) * owners)
        ordered = jnp.concatenate([slots_s[r, at, :] for r in range(share)], axis=0)
        result_s[e] = dot(place_s[...], ordered).astype(BF16)
        out = pltpu.make_async_copy(result_s.at[e], out_ref.at[e], out_sem.at[e])
        out.start()
        outs.append(out)
    for b in range(batches):
        share_map(b).wait_send()
    lax.fori_loop(
        0, batches, lambda b, c: (for_peers(lambda k: away_early(b, k).wait_send()), c)[1], 0
    )
    if quads > early:
        for_peers(lambda k: away_late(k).wait_send())
    for q in range(quads):
        for_peers(lambda k: back(q, k).wait_send())
    for out in outs:
        out.wait()


def on_device(owners, green0, coupling, pattern, broaden, screened, order):
    here = green0.shape[0]
    size = green0.shape[-1]
    points = screened.shape[0]
    share = size // owners
    width = 2 * size
    flat = share * width
    pack = max(p for p in (1, 2, 4) if share % p == 0 and here % (8 // p) == 0)
    quads = share // pack
    many = 8 // pack
    batches = here // many
    early = max(quads - 1, 1)
    green = green0.reshape(here, 2 * size, size)
    gamma = broaden.reshape(here, size, size)

    ticks = np.arange(points)
    angles = (ticks[:, None] * ticks[None, :] % points) * (2.0 * math.pi / points)
    exact = np.concatenate([np.cos(angles), -np.sin(angles)], axis=1)
    high = exact.astype(BF16)
    low = (exact - high.astype(np.float64)).astype(BF16)
    table = jnp.asarray(np.concatenate([high, low], axis=0))
    where = np.arange(points)
    source = (where % owners) * here + where // owners
    unmix = jnp.asarray((source[:, None] == where[None, :]).astype(np.float32).astype(BF16))
    slot = np.arange(size)
    turn = ((slot % owners) * share + slot // owners)[None, :] == slot[:, None]
    turn = jnp.asarray(turn.astype(np.float32).astype(BF16))
    q, o, i, r = np.meshgrid(
        np.arange(quads), np.arange(owners), np.arange(many), np.arange(pack), indexing="ij"
    )
    wanted = (o * share + q * pack + r).reshape(-1)
    owner_of = i.reshape(-1)
    sort = (wanted[None, :, None] == slot[None, None, :]) & (
        owner_of[None, :, None] == np.arange(many)[:, None, None]
    )
    sort = jnp.asarray(sort.astype(np.float32).astype(BF16))

    anywhere = pl.BlockSpec(memory_space=pl.ANY)
    dma = pltpu.SemaphoreType.DMA
    cell = (here, 2 * size, size)
    packed = (owners, batches, 8, quads * width)
    peers = owners - 1
    result = pl.pallas_call(
        functools.partial(fused_kernel, owners, pack, 1.0 / (points * math.sqrt(points))),
        in_specs=[pl.BlockSpec(memory_space=pltpu.SMEM)] + [anywhere] * 9,
        out_specs=anywhere,
        out_shape=jax.ShapeDtypeStruct((here, size, width), BF16),
        scratch_shapes=[
            pltpu.VMEM((size, size), BF16),
            pltpu.VMEM((size, size), BF16),
            pltpu.VMEM((size, size), BF16),
            pltpu.VMEM(cell, BF16),
            pltpu.VMEM((here, size, size), BF16),
            pltpu.VMEM((1, size), jnp.int32),
            pltpu.VMEM(sort.shape, BF16),
            pltpu.VMEM(turn.shape, BF16),
            pltpu.VMEM(table.shape, BF16),
            pltpu.VMEM(unmix.shape, BF16),
            pltpu.VMEM((points * flat // 128, 128), F32),
            pltpu.VMEM(cell, BF16),
            pltpu.VMEM(cell, BF16),
            pltpu.VMEM(cell, F32),
            pltpu.VMEM(cell, BF16),
            pltpu.VMEM(cell, BF16),
            pltpu.VMEM(sort.shape, BF16),
            pltpu.VMEM((size, size), BF16),
            pltpu.VMEM(packed, BF16),
            pltpu.VMEM(packed, BF16),
            pltpu.VMEM((points, flat), F32),
            pltpu.VMEM((owners, here, flat), BF16),
            pltpu.VMEM((owners, here, flat), BF16),
            pltpu.VMEM((share, points, width), BF16),
            pltpu.VMEM((here, size, width), BF16),
            dma((8,)),
            dma((batches,)),
            dma((here,)),
            dma((batches,)),
            dma((batches,)),
            dma((batches, peers)),
            dma((batches, peers)),
            dma((peers,)),
            dma((peers,)),
            dma((quads, peers)),
            dma((quads, peers)),
            dma((batches,)),
            dma((1,)),
            dma((quads,)),
        ],
        compiler_params=pltpu.CompilerParams(collective_id=0, has_side_effects=True),
        name="fused",
    )(
        pattern[0],
        coupling[0],
        green,
        gamma,
        order.reshape(1, size),
        sort,
        turn,
        table,
        unmix,
        screened.reshape(points * flat // 128, 128),
    )
    return result.astype(F32)[:, None]


def solution(mesh):
    return jax.shard_map(
        functools.partial(on_device, mesh.shape["energy"]),
        mesh=mesh,
        in_specs=(
            P("energy", "space", None, None, None),
            P("space", None, None),
            P("space", None, None),
            P("energy", "space", None, None),
            P(None, "space", "energy", None),
            P(),
        ),
        out_specs=P("energy", "space", None, None),
        check_vma=False,
    )
```

```python
import functools
import math

import jax
import jax.numpy as jnp
import numpy as np
from jax import lax
from jax.experimental import pallas as pl
from jax.experimental.pallas import tpu as pltpu
from jax.sharding import PartitionSpec as P

F32 = jnp.float32
BF16 = jnp.bfloat16
PLAIN = ((1,), (0,))
LAST = ((1,), (1,))
FIRST = ((0,), (0,))


def dot(a, b, dims=PLAIN):
    return lax.dot_general(a, b, (dims, ((), ())), preferred_element_type=F32)


def complex_dot(left, right_re, right_im, dims=PLAIN):
    rows = left.shape[0] // 2
    with_re = dot(left, right_re, dims)
    with_im = dot(left, right_im, dims)
    return (with_re[:rows] - with_im[rows:], with_im[:rows] + with_re[rows:])


def stack(pair):
    return jnp.concatenate(pair, axis=0)


def times_i(values):
    half = values.shape[1] // 2
    return jnp.concatenate([-values[:, half:], values[:, :half]], axis=1)


def transform(table, upper, lower):
    both = dot(table, jnp.concatenate([upper, lower], axis=0).astype(BF16))
    points = upper.shape[0]
    return both[:points] + both[points:]


def fused_kernel(
    owners,
    pack,
    scale,
    pattern_ref,
    coupling_ref,
    green_ref,
    gamma_ref,
    order_ref,
    sort_ref,
    turn_ref,
    table_ref,
    unmix_ref,
    screened_ref,
    slots_s,
    place_s,
    pattern_s,
    coupling_s,
    couple_s,
    turned_s,
    green_s,
    gamma_s,
    order_s,
    sort_s,
    turn_s,
    table_s,
    unmix_s,
    screened_s,
    mult_s,
    other_s,
    base_s,
    send_s,
    map_s,
    pick_s,
    mixed_s,
    got_s,
    spectrum_s,
    sigma_s,
    back_s,
    load_sem,
    green_sem,
    map_sent,
    map_landed,
    away_sent,
    away_landed,
    back_sent,
    back_landed,
    own_away,
    own_back,
    ready_sem,
):
    me = lax.axis_index("energy")
    cell = lax.axis_index("space")
    here, both, size = green_s.shape
    rows = both // 2
    width = 2 * size
    share = size // owners
    quads = share // pack
    many = 8 // pack
    batches = here // many
    points = owners * here
    early = max(quads - 1, 1)
    parts = 1 if batches == 1 else 2 if quads == 1 else 3

    def load(n, source, target):
        return pltpu.make_async_copy(source, target, load_sem.at[n])

    def load_green(b):
        at = pl.ds(b * many, many)
        return pltpu.make_async_copy(green_ref.at[at], green_s.at[at], green_sem.at[b])

    loads = [
        load(n, source, target)
        for n, (source, target) in enumerate(
            (
                (pattern_ref, pattern_s),
                (coupling_ref, coupling_s),
                (order_ref, order_s),
                (sort_ref, sort_s),
                (gamma_ref, gamma_s),
                (table_ref, table_s),
                (screened_ref, screened_s),
                (turn_ref, turn_s),
                (unmix_ref, unmix_s),
            )
        )
    ]
    pattern_load, coupling_load, order_load, sort_load, gamma_load, table_load, screened_load, turn_load, unmix_load = loads

    def peer_of(k):
        return lax.rem(me + k, owners)

    def remote(source, target, sent, landed, device):
        return pltpu.make_async_remote_copy(
            src_ref=source,
            dst_ref=target,
            send_sem=sent,
            recv_sem=landed,
            device_id=device,
            device_id_type=pl.DeviceIdType.MESH,
        )

    def share_map(b):
        at = pl.ds(b * many, many)
        return remote(send_s.at[at], map_s.at[at], map_sent.at[b], map_landed.at[b], {"space": 1 - cell})

    def piece(part):
        if part == 0:
            return pl.ds(0, 1), pl.ds(0, quads * width)
        if part == 1:
            return pl.ds(1, batches - 1), pl.ds(0, early * width)
        return pl.ds(1, batches - 1), pl.ds(early * width, (quads - early) * width)

    def away(part, k):
        peer = peer_of(k)
        at, columns = piece(part)
        return remote(
            mixed_s.at[peer, at, :, columns],
            got_s.at[me, at, :, columns],
            away_sent.at[part, k - 1],
            away_landed.at[part, k - 1],
            {"energy": peer},
        )

    def back(q, k):
        peer = peer_of(k)
        columns = pl.ds(q * pack * width, pack * width)
        return remote(
            sigma_s.at[peer, :, columns],
            back_s.at[me, :, columns],
            back_sent.at[q, k - 1],
            back_landed.at[q, k - 1],
            {"energy": peer},
        )

    def keep(part):
        at, columns = piece(part)
        return pltpu.make_async_copy(
            mixed_s.at[me, at, :, columns], got_s.at[me, at, :, columns], own_away.at[part]
        )

    def keep_back(q):
        columns = pl.ds(q * pack * width, pack * width)
        return pltpu.make_async_copy(
            sigma_s.at[me, :, columns], back_s.at[me, :, columns], own_back.at[q]
        )

    def for_peers(action):
        lax.fori_loop(1, owners, lambda k, c: (action(k), c)[1], 0)

    barrier = pltpu.get_barrier_semaphore()
    doubling = owners & (owners - 1) == 0
    near = [1 << n for n in range(owners.bit_length() - 1)] if doubling else range(1, owners)
    rounds = len(near) - 1 if doubling else 0

    def peer_at(distance):
        return jnp.bitwise_xor(me, distance) if doubling else lax.rem(me + distance, owners)

    def pass_on(n):
        if n < rounds:
            pl.semaphore_signal(
                ready_sem.at[n],
                inc=1,
                device_id={"energy": peer_at(near[n])},
                device_id_type=pl.DeviceIdType.MESH,
            )

    def wait_for_round(n):
        if n < rounds:
            pl.semaphore_wait(ready_sem.at[n], 1)

    def greet(device):
        pl.semaphore_signal(barrier, inc=1, device_id=device, device_id_type=pl.DeviceIdType.MESH)

    greet({"space": 1 - cell})
    for distance in near:
        greet({"energy": peer_at(distance)})
    pattern_load.start()
    coupling_load.start()
    for b in range(batches):
        load_green(b).start()
    for each in loads[2:]:
        each.start()
    pl.semaphore_wait(barrier, 1 + len(near))
    pass_on(0)

    tiles = pattern_s.shape[0]
    tile_size = size // tiles
    pattern_load.wait()
    coupling_load.wait()
    lane = lax.broadcasted_iota(jnp.int32, (tile_size, size), 1)
    for i in range(tiles):
        mask = jnp.zeros((tile_size, size), F32)
        for j in range(tiles):
            inside = (lane >= j * tile_size) & (lane < (j + 1) * tile_size)
            mask = jnp.where(inside, pattern_s[i, j].astype(F32), mask)
        at = slice(i * tile_size, (i + 1) * tile_size)
        couple_s[at, :] = (coupling_s[at, :].astype(F32) * mask).astype(BF16)

    @pl.when(cell == 1)
    def _():
        turned_s[...] = jnp.transpose(couple_s[...].astype(F32)).astype(BF16)

    def born(b):
        load_green(b).wait()
        batch = [b * many + i for i in range(many)]

        @pl.when(cell == 0)
        def _():
            couple = couple_s[...]
            green = [green_s[e] for e in batch]
            factor = [dot(g, couple).astype(BF16) for g in green]
            moved = [
                stack(complex_dot(f, g[:rows], g[rows:])).astype(BF16) for f, g in zip(factor, green)
            ]
            for e, f, g, m in zip(batch, factor, green, moved):
                base = g.astype(F32) + stack(complex_dot(m, f[:rows], f[rows:], LAST))
                base_s[e] = base
                send_s[e] = base.astype(BF16)
                mult_s[e] = g
                other_s[e] = g

        @pl.when(cell == 1)
        def _():
            couple = couple_s[...]
            turned = turned_s[...]
            green = [green_s[e] for e in batch]
            flipped = [
                stack((dot(turned, g[:rows], LAST), dot(turned, g[rows:], LAST))).astype(BF16)
                for g in green
            ]
            for e, f in zip(batch, flipped):
                send_s[e] = dot(f, couple).astype(BF16)
                other_s[e] = f
            for e, g in zip(batch, green):
                mult_s[e] = dot(g, couple).astype(BF16)
                base_s[e] = g.astype(F32)

    def lesser(b):
        batch = [b * many + i for i in range(many)]
        mult = [mult_s[e] for e in batch]
        other = [other_s[e] for e in batch]
        moved = [
            stack(complex_dot(m, map_s[e, :rows], map_s[e, rows:])).astype(BF16)
            for e, m in zip(batch, mult)
        ]
        full = [
            (base_s[e] + stack(complex_dot(m, o[:rows], o[rows:]))).astype(BF16)
            for e, m, o in zip(batch, moved, other)
        ]
        weighted = [dot(f, gamma_s[e]).astype(BF16) for e, f in zip(batch, full)]
        found = [
            (
                dot(w[:rows], stack((f[rows:], f[:rows])), LAST)
                + dot(w[rows:], stack((-f[:rows], f[rows:])), LAST)
            ).astype(BF16)
            for w, f in zip(weighted, full)
        ]
        block = 8 * owners
        for q in range(quads):
            at = slice(q * block, (q + 1) * block)
            mixed = sum(dot(pick_s[i, at], found[i]) for i in range(many))
            mixed_s[:, b, :, q * width : (q + 1) * width] = mixed.reshape(owners, 8, width).astype(BF16)

    born(0)
    share_map(0).start()
    wait_for_round(0)
    pass_on(1)
    if batches > 1:
        born(1)
        share_map(1).start()
    wait_for_round(1)
    pass_on(2)
    order_load.wait()
    sort_load.wait()
    ids = lax.broadcasted_iota(jnp.int32, (size, size), 0)
    place = jnp.where(ids == order_s[...], 1.0, 0.0).astype(BF16)
    for i in range(many):
        pick_s[i] = dot(sort_s[i], place, LAST).astype(BF16)
    gamma_load.wait()

    for b in range(batches):
        share_map(b).wait_recv()
        lesser(b)
        if b == 0:
            for n in range(2, rounds):
                wait_for_round(n)
                pass_on(n + 1)
            for_peers(lambda k: away(0, k).start())
            keep(0).start()
        if b + 2 < batches:
            born(b + 2)
            share_map(b + 2).start()
    for part in range(1, parts):
        for_peers(lambda k: away(part, k).start())
        keep(part).start()
    turn_load.wait()
    place_s[...] = dot(place, turn_s[...]).astype(BF16)
    table_load.wait()
    screened_load.wait()
    unmix_load.wait()
    table = table_s[...]
    pieces = width // 128
    for r in range(share):
        values = jnp.concatenate(
            [
                screened_s[pl.ds(r * pieces + c, points, stride=share * pieces), :]
                for c in range(pieces)
            ],
            axis=1,
        )
        spectrum_s[:, r * width : (r + 1) * width] = transform(table, values, times_i(values)) * scale

    half = width // 2
    row_ids = lax.broadcasted_iota(jnp.int32, (points, points * pack), 0)
    column_ids = lax.broadcasted_iota(jnp.int32, (points, points * pack), 1)
    for q in range(quads):
        for part in range(parts):
            if q == (early if part == 2 else 0):
                for_peers(lambda k: away(part, k).wait_recv())
                keep(part).wait()
        packed = got_s[:, :, :, q * width : (q + 1) * width].astype(F32)
        packed = packed.reshape(points * pack, width).astype(BF16)
        for r in range(pack):
            if pack == 1:
                values = packed.astype(F32)
            else:
                chosen = jnp.where(column_ids == row_ids * pack + r, 1.0, 0.0).astype(BF16)
                values = dot(chosen, packed)
            at = slice((q * pack + r) * width, (q * pack + r + 1) * width)
            kernel = spectrum_s[:, at]
            spectrum = transform(table, values, times_i(values))
            kernel_re = jnp.concatenate([kernel[:, :half], kernel[:, :half]], axis=1)
            kernel_im = jnp.concatenate([kernel[:, half:], kernel[:, half:]], axis=1)
            product = spectrum * kernel_re + times_i(spectrum) * kernel_im
            found = transform(table, times_i(product), product)
            sigma_s[:, :, at] = found.reshape(owners, here, width).astype(BF16)
        for_peers(lambda k: back(q, k).start())
        keep_back(q).start()

    unmix = unmix_s[...]
    for q in range(quads):
        for_peers(lambda k: back(q, k).wait_recv())
        keep_back(q).wait()
        for r in range(q * pack, (q + 1) * pack):
            values = back_s[:, :, r * width : (r + 1) * width].astype(F32)
            values = values.reshape(points, width).astype(BF16)
            slots_s[r] = dot(unmix, values).astype(BF16)
    for b in range(batches):
        share_map(b).wait_send()
    for part in range(parts):
        for_peers(lambda k: away(part, k).wait_send())
    for q in range(quads):
        for_peers(lambda k: back(q, k).wait_send())


def restore_kernel(slots_ref, place_ref, out_ref, result_s, out_sem):
    here, size, width = result_s.shape
    share, points, _ = slots_ref.shape
    owners = points // here
    place = place_ref[...]
    outs = []
    for e in range(here):
        at = slice(e * owners, (e + 1) * owners)
        ordered = jnp.concatenate([slots_ref[r, at, :] for r in range(share)], axis=0)
        result_s[e] = dot(place, ordered)
        out = pltpu.make_async_copy(result_s.at[e], out_ref.at[e], out_sem.at[e])
        out.start()
        outs.append(out)
    for out in outs:
        out.wait()


def on_device(owners, green0, coupling, pattern, broaden, screened, order):
    here = green0.shape[0]
    size = green0.shape[-1]
    points = screened.shape[0]
    share = size // owners
    width = 2 * size
    flat = share * width
    pack = max(p for p in (1, 2, 4) if share % p == 0 and here % (8 // p) == 0)
    quads = share // pack
    many = 8 // pack
    batches = here // many
    early = max(quads - 1, 1)
    green = green0.reshape(here, 2 * size, size)
    gamma = broaden.reshape(here, size, size)

    ticks = np.arange(points)
    angles = (ticks[:, None] * ticks[None, :] % points) * (2.0 * math.pi / points)
    exact = np.concatenate([np.cos(angles), -np.sin(angles)], axis=1)
    high = exact.astype(BF16)
    low = (exact - high.astype(np.float64)).astype(BF16)
    table = jnp.asarray(np.concatenate([high, low], axis=0))
    where = np.arange(points)
    source = (where % owners) * here + where // owners
    unmix = jnp.asarray((source[:, None] == where[None, :]).astype(np.float32).astype(BF16))
    slot = np.arange(size)
    turn = ((slot % owners) * share + slot // owners)[None, :] == slot[:, None]
    turn = jnp.asarray(turn.astype(np.float32).astype(BF16))
    q, o, i, r = np.meshgrid(
        np.arange(quads), np.arange(owners), np.arange(many), np.arange(pack), indexing="ij"
    )
    wanted = (o * share + q * pack + r).reshape(-1)
    owner_of = i.reshape(-1)
    sort = (wanted[None, :, None] == slot[None, None, :]) & (
        owner_of[None, :, None] == np.arange(many)[:, None, None]
    )
    sort = jnp.asarray(sort.astype(np.float32).astype(BF16))

    anywhere = pl.BlockSpec(memory_space=pltpu.HBM)
    dma = pltpu.SemaphoreType.DMA
    cell = (here, 2 * size, size)
    packed = (owners, batches, 8, quads * width)
    peers = owners - 1
    vmem = pl.BlockSpec(memory_space=pltpu.VMEM)
    slots, place = pl.pallas_call(
        functools.partial(fused_kernel, owners, pack, 1.0 / (points * math.sqrt(points))),
        in_specs=[anywhere] * 10,
        out_specs=[vmem, vmem],
        out_shape=[
            jax.ShapeDtypeStruct((share, points, width), BF16),
            jax.ShapeDtypeStruct((size, size), BF16),
        ],
        scratch_shapes=[
            pltpu.SMEM(pattern.shape[1:], jnp.int32),
            pltpu.VMEM((size, size), BF16),
            pltpu.VMEM((size, size), BF16),
            pltpu.VMEM((size, size), BF16),
            pltpu.VMEM(cell, BF16),
            pltpu.VMEM((here, size, size), BF16),
            pltpu.VMEM((1, size), jnp.int32),
            pltpu.VMEM(sort.shape, BF16),
            pltpu.VMEM(turn.shape, BF16),
            pltpu.VMEM(table.shape, BF16),
            pltpu.VMEM(unmix.shape, BF16),
            pltpu.VMEM((points * flat // 128, 128), F32),
            pltpu.VMEM(cell, BF16),
            pltpu.VMEM(cell, BF16),
            pltpu.VMEM(cell, F32),
            pltpu.VMEM(cell, BF16),
            pltpu.VMEM(cell, BF16),
            pltpu.VMEM(sort.shape, BF16),
            pltpu.VMEM(packed, BF16),
            pltpu.VMEM(packed, BF16),
            pltpu.VMEM((points, flat), F32),
            pltpu.VMEM((owners, here, flat), BF16),
            pltpu.VMEM((owners, here, flat), BF16),
            dma((9,)),
            dma((batches,)),
            dma((batches,)),
            dma((batches,)),
            dma((3, peers)),
            dma((3, peers)),
            dma((quads, peers)),
            dma((quads, peers)),
            dma((3,)),
            dma((quads,)),
            pltpu.SemaphoreType.REGULAR((owners.bit_length(),)),
        ],
        compiler_params=pltpu.CompilerParams(
            collective_id=0, has_side_effects=True, vmem_limit_bytes=56 << 20
        ),
        name="fused",
    )(*(pltpu.with_memory_space_constraint(value, pltpu.HBM) for value in (
        pattern[0],
        coupling[0],
        green,
        gamma,
        order.reshape(1, size),
        sort,
        turn,
        table,
        unmix,
        screened.reshape(points * flat // 128, 128),
    )))
    result = pl.pallas_call(
        restore_kernel,
        in_specs=[vmem, vmem],
        out_specs=anywhere,
        out_shape=jax.ShapeDtypeStruct((here, size, width), F32),
        scratch_shapes=[pltpu.VMEM((here, size, width), F32), dma((here,))],
        compiler_params=pltpu.CompilerParams(vmem_limit_bytes=16 << 20),
        name="restore",
    )(slots, place)
    return result[:, None]


def solution(mesh):
    return jax.shard_map(
        functools.partial(on_device, mesh.shape["energy"]),
        mesh=mesh,
        in_specs=(
            P("energy", "space", None, None, None),
            P("space", None, None),
            P("space", None, None),
            P("energy", "space", None, None),
            P(None, "space", "energy", None),
            P(),
        ),
        out_specs=P("energy", "space", None, None),
        check_vma=False,
    )
```

```python
import functools
import math

import jax
import jax.numpy as jnp
import numpy as np
from jax import lax
from jax.experimental import pallas as pl
from jax.experimental.pallas import tpu as pltpu
from jax.sharding import PartitionSpec as P

F32 = jnp.float32
BF16 = jnp.bfloat16
PLAIN = ((1,), (0,))
LAST = ((1,), (1,))
FIRST = ((0,), (0,))


def dot(a, b, dims=PLAIN):
    return lax.dot_general(a, b, (dims, ((), ())), preferred_element_type=F32)


def complex_dot(left, right_re, right_im, dims=PLAIN):
    rows = left.shape[0] // 2
    with_re = dot(left, right_re, dims)
    with_im = dot(left, right_im, dims)
    return (with_re[:rows] - with_im[rows:], with_im[:rows] + with_re[rows:])


def stack(pair):
    return jnp.concatenate(pair, axis=0)


def times_i(values):
    half = values.shape[1] // 2
    return jnp.concatenate([-values[:, half:], values[:, :half]], axis=1)


def transform(table, upper, lower):
    both = dot(table, jnp.concatenate([upper, lower], axis=0).astype(BF16))
    points = upper.shape[0]
    return both[:points] + both[points:]


def fused_kernel(
    owners,
    pack,
    scale,
    pattern_ref,
    coupling_ref,
    green_ref,
    gamma_ref,
    order_ref,
    sort_ref,
    turn_ref,
    table_ref,
    unmix_ref,
    screened_ref,
    slots_s,
    place_s,
    pattern_s,
    coupling_s,
    couple_s,
    turned_s,
    green_s,
    gamma_s,
    order_s,
    sort_s,
    turn_s,
    table_s,
    unmix_s,
    screened_s,
    mult_s,
    other_s,
    base_s,
    send_s,
    map_s,
    pick_s,
    mixed_s,
    got_s,
    spectrum_s,
    sigma_s,
    back_s,
    load_sem,
    green_sem,
    map_sent,
    map_landed,
    away_sent,
    away_landed,
    back_sent,
    back_landed,
    own_away,
    own_back,
    ready_sem,
):
    me = lax.axis_index("energy")
    cell = lax.axis_index("space")
    here, both, size = green_s.shape
    rows = both // 2
    width = 2 * size
    share = size // owners
    quads = share // pack
    many = 8 // pack
    batches = here // many
    points = owners * here
    early = max(quads - 1, 1)
    parts = 1 if batches == 1 else 2 if quads == 1 else 3

    def load(n, source, target):
        return pltpu.make_async_copy(source, target, load_sem.at[n])

    def load_green(b):
        at = pl.ds(b * many, many)
        return pltpu.make_async_copy(green_ref.at[at], green_s.at[at], green_sem.at[b])

    loads = [
        load(n, source, target)
        for n, (source, target) in enumerate(
            (
                (pattern_ref, pattern_s),
                (coupling_ref, coupling_s),
                (order_ref, order_s),
                (sort_ref, sort_s),
                (gamma_ref, gamma_s),
                (table_ref, table_s),
                (screened_ref, screened_s),
                (turn_ref, turn_s),
                (unmix_ref, unmix_s),
            )
        )
    ]
    pattern_load, coupling_load, order_load, sort_load, gamma_load, table_load, screened_load, turn_load, unmix_load = loads

    doubling = owners & (owners - 1) == 0
    low = 1 << (owners.bit_length() - 1) // 2 if doubling else 1

    def peer_of(k):
        return lax.rem(me + k, owners)

    def partner_of(k):
        return jnp.bitwise_xor(me, k) if doubling else peer_of(k)

    def remote(source, target, sent, landed, device):
        return pltpu.make_async_remote_copy(
            src_ref=source,
            dst_ref=target,
            send_sem=sent,
            recv_sem=landed,
            device_id=device,
            device_id_type=pl.DeviceIdType.MESH,
        )

    def share_map(b):
        at = pl.ds(b * many, many)
        return remote(send_s.at[at], map_s.at[at], map_sent.at[b], map_landed.at[b], {"space": 1 - cell})

    def piece(part):
        if part == 0:
            return pl.ds(0, 1), pl.ds(0, quads * width)
        if part == 1:
            return pl.ds(1, batches - 1), pl.ds(0, early * width)
        return pl.ds(1, batches - 1), pl.ds(early * width, (quads - early) * width)

    def away(part, k):
        peer = peer_of(k) if part else partner_of(k)
        at, columns = piece(part)
        return remote(
            mixed_s.at[peer, at, :, columns],
            got_s.at[me, at, :, columns],
            away_sent.at[part, k - 1],
            away_landed.at[part, k - 1],
            {"energy": peer},
        )

    def back(q, k):
        peer = peer_of(k)
        columns = pl.ds(q * pack * width, pack * width)
        return remote(
            sigma_s.at[peer, :, columns],
            back_s.at[me, :, columns],
            back_sent.at[q, k - 1],
            back_landed.at[q, k - 1],
            {"energy": peer},
        )

    def keep(part):
        at, columns = piece(part)
        return pltpu.make_async_copy(
            mixed_s.at[me, at, :, columns], got_s.at[me, at, :, columns], own_away.at[part]
        )

    def keep_back(q):
        columns = pl.ds(q * pack * width, pack * width)
        return pltpu.make_async_copy(
            sigma_s.at[me, :, columns], back_s.at[me, :, columns], own_back.at[q]
        )

    def for_peers(action):
        lax.fori_loop(1, owners, lambda k, c: (action(k), c)[1], 0)

    barrier = pltpu.get_barrier_semaphore()
    near = list(range(1, low)) + list(range(low, owners, low))

    def greet(device):
        pl.semaphore_signal(barrier, inc=1, device_id=device, device_id_type=pl.DeviceIdType.MESH)

    def say_ready(d):
        pl.semaphore_signal(
            ready_sem.at[d],
            inc=1,
            device_id={"energy": partner_of(d)},
            device_id_type=pl.DeviceIdType.MESH,
        )

    def first_away(d):
        if d:
            pl.semaphore_wait(ready_sem.at[d], 1)
        lax.fori_loop(
            0 if d else 1, owners // low, lambda j, c: (away(0, d + low * j).start(), c)[1], 0
        )

    greet({"space": 1 - cell})
    for distance in near:
        greet({"energy": partner_of(distance)})
    pattern_load.start()
    coupling_load.start()
    for b in range(min(2, batches)):
        load_green(b).start()
    for each in (order_load, sort_load, gamma_load):
        each.start()

    tiles = pattern_s.shape[0]
    tile_size = size // tiles
    pattern_load.wait()
    coupling_load.wait()
    lane = lax.broadcasted_iota(jnp.int32, (tile_size, size), 1)
    for i in range(tiles):
        mask = jnp.zeros((tile_size, size), F32)
        for j in range(tiles):
            inside = (lane >= j * tile_size) & (lane < (j + 1) * tile_size)
            mask = jnp.where(inside, pattern_s[i, j].astype(F32), mask)
        at = slice(i * tile_size, (i + 1) * tile_size)
        couple_s[at, :] = (coupling_s[at, :].astype(F32) * mask).astype(BF16)

    @pl.when(cell == 1)
    def _():
        turned_s[...] = jnp.transpose(couple_s[...].astype(F32)).astype(BF16)

    def born(b):
        load_green(b).wait()
        batch = [b * many + i for i in range(many)]

        @pl.when(cell == 0)
        def _():
            couple = couple_s[...]
            green = [green_s[e] for e in batch]
            factor = [dot(g, couple).astype(BF16) for g in green]
            moved = [
                stack(complex_dot(f, g[:rows], g[rows:])).astype(BF16) for f, g in zip(factor, green)
            ]
            for e, f, g, m in zip(batch, factor, green, moved):
                base = g.astype(F32) + stack(complex_dot(m, f[:rows], f[rows:], LAST))
                base_s[e] = base
                send_s[e] = base.astype(BF16)
                mult_s[e] = g
                other_s[e] = g

        @pl.when(cell == 1)
        def _():
            couple = couple_s[...]
            turned = turned_s[...]
            green = [green_s[e] for e in batch]
            flipped = [
                stack((dot(turned, g[:rows], LAST), dot(turned, g[rows:], LAST))).astype(BF16)
                for g in green
            ]
            for e, f in zip(batch, flipped):
                send_s[e] = dot(f, couple).astype(BF16)
                other_s[e] = f
            for e, g in zip(batch, green):
                mult_s[e] = dot(g, couple).astype(BF16)
                base_s[e] = g.astype(F32)

    def lesser(b):
        batch = [b * many + i for i in range(many)]
        mult = [mult_s[e] for e in batch]
        other = [other_s[e] for e in batch]
        moved = [
            stack(complex_dot(m, map_s[e, :rows], map_s[e, rows:])).astype(BF16)
            for e, m in zip(batch, mult)
        ]
        full = [
            (base_s[e] + stack(complex_dot(m, o[:rows], o[rows:]))).astype(BF16)
            for e, m, o in zip(batch, moved, other)
        ]
        weighted = [dot(f, gamma_s[e]).astype(BF16) for e, f in zip(batch, full)]
        found = [
            (
                dot(w[:rows], stack((f[rows:], f[:rows])), LAST)
                + dot(w[rows:], stack((-f[:rows], f[rows:])), LAST)
            ).astype(BF16)
            for w, f in zip(weighted, full)
        ]
        block = 8 * owners
        for q in range(quads):
            at = slice(q * block, (q + 1) * block)
            mixed = sum(dot(pick_s[i, at], found[i]) for i in range(many))
            mixed_s[:, b, :, q * width : (q + 1) * width] = mixed.reshape(owners, 8, width).astype(BF16)

    born(0)
    pl.semaphore_wait(barrier, 1 + len(near))
    share_map(0).start()
    for d in range(1, low):
        say_ready(d)
    for b in range(2, batches):
        load_green(b).start()
    for each in (screened_load, table_load, turn_load, unmix_load):
        each.start()
    if batches > 1:
        born(1)
        share_map(1).start()
    order_load.wait()
    sort_load.wait()
    ids = lax.broadcasted_iota(jnp.int32, (size, size), 0)
    place = jnp.where(ids == order_s[...], 1.0, 0.0).astype(BF16)
    for i in range(many):
        pick_s[i] = dot(sort_s[i], place, LAST).astype(BF16)
    gamma_load.wait()

    for b in range(batches):
        share_map(b).wait_recv()
        lesser(b)
        if b == 0:
            for d in range(low):
                first_away(d)
            keep(0).start()
        if b + 2 < batches:
            born(b + 2)
            share_map(b + 2).start()
    for part in range(1, parts):
        for_peers(lambda k: away(part, k).start())
        keep(part).start()
    turn_load.wait()
    place_s[...] = dot(place, turn_s[...]).astype(BF16)
    table_load.wait()
    screened_load.wait()
    unmix_load.wait()
    table = table_s[...]
    pieces = width // 128
    for r in range(share):
        values = jnp.concatenate(
            [
                screened_s[pl.ds(r * pieces + c, points, stride=share * pieces), :]
                for c in range(pieces)
            ],
            axis=1,
        )
        spectrum_s[:, r * width : (r + 1) * width] = transform(table, values, times_i(values)) * scale

    half = width // 2
    row_ids = lax.broadcasted_iota(jnp.int32, (points, points * pack), 0)
    column_ids = lax.broadcasted_iota(jnp.int32, (points, points * pack), 1)
    for q in range(quads):
        for part in range(parts):
            if q == (early if part == 2 else 0):
                for_peers(lambda k: away(part, k).wait_recv())
                keep(part).wait()
        packed = got_s[:, :, :, q * width : (q + 1) * width].astype(F32)
        packed = packed.reshape(points * pack, width).astype(BF16)
        for r in range(pack):
            if pack == 1:
                values = packed.astype(F32)
            else:
                chosen = jnp.where(column_ids == row_ids * pack + r, 1.0, 0.0).astype(BF16)
                values = dot(chosen, packed)
            at = slice((q * pack + r) * width, (q * pack + r + 1) * width)
            kernel = spectrum_s[:, at]
            spectrum = transform(table, values, times_i(values))
            kernel_re = jnp.concatenate([kernel[:, :half], kernel[:, :half]], axis=1)
            kernel_im = jnp.concatenate([kernel[:, half:], kernel[:, half:]], axis=1)
            product = spectrum * kernel_re + times_i(spectrum) * kernel_im
            found = transform(table, times_i(product), product)
            sigma_s[:, :, at] = found.reshape(owners, here, width).astype(BF16)
        for_peers(lambda k: back(q, k).start())
        keep_back(q).start()

    unmix = unmix_s[...]
    for q in range(quads):
        for_peers(lambda k: back(q, k).wait_recv())
        keep_back(q).wait()
        for r in range(q * pack, (q + 1) * pack):
            values = back_s[:, :, r * width : (r + 1) * width].astype(F32)
            values = values.reshape(points, width).astype(BF16)
            slots_s[r] = dot(unmix, values).astype(BF16)
    for b in range(batches):
        share_map(b).wait_send()
    for part in range(parts):
        for_peers(lambda k: away(part, k).wait_send())
    for q in range(quads):
        for_peers(lambda k: back(q, k).wait_send())


def restore_kernel(slots_ref, place_ref, out_ref, result_s, out_sem):
    here, size, width = result_s.shape
    share, points, _ = slots_ref.shape
    owners = points // here
    place = place_ref[...]
    outs = []
    for e in range(here):
        at = slice(e * owners, (e + 1) * owners)
        ordered = jnp.concatenate([slots_ref[r, at, :] for r in range(share)], axis=0)
        result_s[e] = dot(place, ordered)
        out = pltpu.make_async_copy(result_s.at[e], out_ref.at[e], out_sem.at[e])
        out.start()
        outs.append(out)
    for out in outs:
        out.wait()


def on_device(owners, green0, coupling, pattern, broaden, screened, order):
    here = green0.shape[0]
    size = green0.shape[-1]
    points = screened.shape[0]
    share = size // owners
    width = 2 * size
    flat = share * width
    pack = max(p for p in (1, 2, 4) if share % p == 0 and here % (8 // p) == 0)
    quads = share // pack
    many = 8 // pack
    batches = here // many
    early = max(quads - 1, 1)
    green = green0.reshape(here, 2 * size, size)
    gamma = broaden.reshape(here, size, size)

    ticks = np.arange(points)
    angles = (ticks[:, None] * ticks[None, :] % points) * (2.0 * math.pi / points)
    exact = np.concatenate([np.cos(angles), -np.sin(angles)], axis=1)
    high = exact.astype(BF16)
    low = (exact - high.astype(np.float64)).astype(BF16)
    table = jnp.asarray(np.concatenate([high, low], axis=0))
    where = np.arange(points)
    source = (where % owners) * here + where // owners
    unmix = jnp.asarray((source[:, None] == where[None, :]).astype(np.float32).astype(BF16))
    slot = np.arange(size)
    turn = ((slot % owners) * share + slot // owners)[None, :] == slot[:, None]
    turn = jnp.asarray(turn.astype(np.float32).astype(BF16))
    q, o, i, r = np.meshgrid(
        np.arange(quads), np.arange(owners), np.arange(many), np.arange(pack), indexing="ij"
    )
    wanted = (o * share + q * pack + r).reshape(-1)
    owner_of = i.reshape(-1)
    sort = (wanted[None, :, None] == slot[None, None, :]) & (
        owner_of[None, :, None] == np.arange(many)[:, None, None]
    )
    sort = jnp.asarray(sort.astype(np.float32).astype(BF16))

    anywhere = pl.BlockSpec(memory_space=pltpu.HBM)
    dma = pltpu.SemaphoreType.DMA
    cell = (here, 2 * size, size)
    packed = (owners, batches, 8, quads * width)
    peers = owners - 1
    vmem = pl.BlockSpec(memory_space=pltpu.VMEM)
    slots, place = pl.pallas_call(
        functools.partial(fused_kernel, owners, pack, 1.0 / (points * math.sqrt(points))),
        in_specs=[anywhere] * 10,
        out_specs=[vmem, vmem],
        out_shape=[
            jax.ShapeDtypeStruct((share, points, width), BF16),
            jax.ShapeDtypeStruct((size, size), BF16),
        ],
        scratch_shapes=[
            pltpu.SMEM(pattern.shape[1:], jnp.int32),
            pltpu.VMEM((size, size), BF16),
            pltpu.VMEM((size, size), BF16),
            pltpu.VMEM((size, size), BF16),
            pltpu.VMEM(cell, BF16),
            pltpu.VMEM((here, size, size), BF16),
            pltpu.VMEM((1, size), jnp.int32),
            pltpu.VMEM(sort.shape, BF16),
            pltpu.VMEM(turn.shape, BF16),
            pltpu.VMEM(table.shape, BF16),
            pltpu.VMEM(unmix.shape, BF16),
            pltpu.VMEM((points * flat // 128, 128), F32),
            pltpu.VMEM(cell, BF16),
            pltpu.VMEM(cell, BF16),
            pltpu.VMEM(cell, F32),
            pltpu.VMEM(cell, BF16),
            pltpu.VMEM(cell, BF16),
            pltpu.VMEM(sort.shape, BF16),
            pltpu.VMEM(packed, BF16),
            pltpu.VMEM(packed, BF16),
            pltpu.VMEM((points, flat), F32),
            pltpu.VMEM((owners, here, flat), BF16),
            pltpu.VMEM((owners, here, flat), BF16),
            dma((9,)),
            dma((batches,)),
            dma((batches,)),
            dma((batches,)),
            dma((3, peers)),
            dma((3, peers)),
            dma((quads, peers)),
            dma((quads, peers)),
            dma((3,)),
            dma((quads,)),
            pltpu.SemaphoreType.REGULAR((owners.bit_length(),)),
        ],
        compiler_params=pltpu.CompilerParams(
            collective_id=0, has_side_effects=True, vmem_limit_bytes=44 << 20
        ),
        name="fused",
    )(*(pltpu.with_memory_space_constraint(value, pltpu.HBM) for value in (
        pattern[0],
        coupling[0],
        green,
        gamma,
        order.reshape(1, size),
        sort,
        turn,
        table,
        unmix,
        screened.reshape(points * flat // 128, 128),
    )))
    result = pl.pallas_call(
        restore_kernel,
        in_specs=[vmem, vmem],
        out_specs=anywhere,
        out_shape=jax.ShapeDtypeStruct((here, size, width), F32),
        scratch_shapes=[pltpu.VMEM((here, size, width), F32), dma((here,))],
        compiler_params=pltpu.CompilerParams(vmem_limit_bytes=16 << 20),
        name="restore",
    )(slots, place)
    return result[:, None]


def solution(mesh):
    return jax.shard_map(
        functools.partial(on_device, mesh.shape["energy"]),
        mesh=mesh,
        in_specs=(
            P("energy", "space", None, None, None),
            P("space", None, None),
            P("space", None, None),
            P("energy", "space", None, None),
            P(None, "space", "energy", None),
            P(),
        ),
        out_specs=P("energy", "space", None, None),
        check_vma=False,
    )
```

```python
import functools
import math

import jax
import jax.numpy as jnp
import numpy as np
from jax import lax
from jax.experimental import pallas as pl
from jax.experimental.pallas import tpu as pltpu
from jax.sharding import PartitionSpec as P

F32 = jnp.float32
BF16 = jnp.bfloat16
PLAIN = ((1,), (0,))
LAST = ((1,), (1,))
FIRST = ((0,), (0,))


def dot(a, b, dims=PLAIN):
    return lax.dot_general(a, b, (dims, ((), ())), preferred_element_type=F32)


def complex_dot(left, right_re, right_im, dims=PLAIN):
    rows = left.shape[0] // 2
    with_re = dot(left, right_re, dims)
    with_im = dot(left, right_im, dims)
    return (with_re[:rows] - with_im[rows:], with_im[:rows] + with_re[rows:])


def stack(pair):
    return jnp.concatenate(pair, axis=0)


def times_i(values):
    half = values.shape[1] // 2
    return jnp.concatenate([-values[:, half:], values[:, :half]], axis=1)


def transform(table, upper, lower):
    both = dot(table, jnp.concatenate([upper, lower], axis=0).astype(BF16))
    points = upper.shape[0]
    return both[:points] + both[points:]


def fused_kernel(
    owners,
    pack,
    scale,
    pattern_ref,
    coupling_ref,
    green_ref,
    gamma_ref,
    order_ref,
    sort_ref,
    turn_ref,
    table_ref,
    unmix_ref,
    screened_ref,
    slots_s,
    place_s,
    pattern_s,
    coupling_s,
    couple_s,
    turned_s,
    green_s,
    gamma_s,
    order_s,
    sort_s,
    turn_s,
    table_s,
    unmix_s,
    screened_s,
    mult_s,
    other_s,
    base_s,
    send_s,
    map_s,
    pick_s,
    mixed_s,
    got_s,
    spectrum_s,
    sigma_s,
    back_s,
    load_sem,
    green_sem,
    map_sent,
    map_landed,
    away_sent,
    away_landed,
    back_sent,
    back_landed,
    ready_sem,
):
    me = lax.axis_index("energy")
    cell = lax.axis_index("space")
    here, both, size = green_s.shape
    rows = both // 2
    width = 2 * size
    share = size // owners
    quads = share // pack
    many = 8 // pack
    batches = here // many
    points = owners * here
    early = max(quads - 1, 1)
    parts = 1 if batches == 1 else 2 if quads == 1 else 3

    def load(n, source, target):
        return pltpu.make_async_copy(source, target, load_sem.at[n])

    def load_green(b):
        at = pl.ds(b * many, many)
        return pltpu.make_async_copy(green_ref.at[at], green_s.at[at], green_sem.at[b])

    loads = [
        load(n, source, target)
        for n, (source, target) in enumerate(
            (
                (pattern_ref, pattern_s),
                (coupling_ref, coupling_s),
                (order_ref, order_s),
                (sort_ref, sort_s),
                (gamma_ref, gamma_s),
                (table_ref, table_s),
                (screened_ref, screened_s),
                (turn_ref, turn_s),
                (unmix_ref, unmix_s),
            )
        )
    ]
    pattern_load, coupling_load, order_load, sort_load, gamma_load, table_load, screened_load, turn_load, unmix_load = loads

    doubling = owners & (owners - 1) == 0
    low = 1 << (owners.bit_length() - 1) // 2 if doubling else 1

    def peer_of(k):
        return lax.rem(me + k, owners)

    def partner_of(k):
        return jnp.bitwise_xor(me, k) if doubling else peer_of(k)

    def remote(source, target, sent, landed, device):
        return pltpu.make_async_remote_copy(
            src_ref=source,
            dst_ref=target,
            send_sem=sent,
            recv_sem=landed,
            device_id=device,
            device_id_type=pl.DeviceIdType.MESH,
        )

    def share_map(b):
        at = pl.ds(b * many, many)
        return remote(send_s.at[at], map_s.at[at], map_sent.at[b], map_landed.at[b], {"space": 1 - cell})

    def piece(part):
        if part == 0:
            return pl.ds(0, 1), pl.ds(0, quads * width)
        if part == 1:
            return pl.ds(1, batches - 1), pl.ds(0, early * width)
        return pl.ds(1, batches - 1), pl.ds(early * width, (quads - early) * width)

    def away(part, k):
        peer = peer_of(k) if part else partner_of(k)
        at, columns = piece(part)
        return remote(
            mixed_s.at[peer, at, :, columns],
            got_s.at[me, at, :, columns],
            away_sent.at[part],
            away_landed.at[part],
            {"energy": peer},
        )

    def back(q, k):
        peer = peer_of(k)
        columns = pl.ds(q * pack * width, pack * width)
        return remote(
            sigma_s.at[peer, :, columns],
            back_s.at[me, :, columns],
            back_sent.at[q],
            back_landed.at[q],
            {"energy": peer},
        )

    def keep(part):
        at, columns = piece(part)
        return pltpu.make_async_copy(
            mixed_s.at[me, at, :, columns], got_s.at[me, at, :, columns], away_landed.at[part]
        )

    def keep_back(q):
        columns = pl.ds(q * pack * width, pack * width)
        return pltpu.make_async_copy(
            sigma_s.at[me, :, columns], back_s.at[me, :, columns], back_landed.at[q]
        )

    def all_away(part, count, sem):
        at, columns = piece(part)
        some = pl.ds(0, count)
        return pltpu.make_async_copy(
            mixed_s.at[some, at, :, columns], got_s.at[some, at, :, columns], sem.at[part]
        )

    def all_back(q, count, sem):
        columns = pl.ds(q * pack * width, pack * width)
        some = pl.ds(0, count)
        return pltpu.make_async_copy(
            sigma_s.at[some, :, columns], back_s.at[some, :, columns], sem.at[q]
        )

    def for_peers(action):
        lax.fori_loop(1, owners, lambda k, c: (action(k), c)[1], 0)

    barrier = pltpu.get_barrier_semaphore()
    near = list(range(1, low)) + list(range(low, owners, low))

    def greet(device):
        pl.semaphore_signal(barrier, inc=1, device_id=device, device_id_type=pl.DeviceIdType.MESH)

    def say_ready(d):
        pl.semaphore_signal(
            ready_sem.at[d],
            inc=1,
            device_id={"energy": partner_of(d)},
            device_id_type=pl.DeviceIdType.MESH,
        )

    def first_away(d):
        if d:
            pl.semaphore_wait(ready_sem.at[d], 1)
        lax.fori_loop(
            0 if d else 1, owners // low, lambda j, c: (away(0, d + low * j).start(), c)[1], 0
        )

    greet({"space": 1 - cell})
    for distance in near:
        greet({"energy": partner_of(distance)})
    pattern_load.start()
    coupling_load.start()
    for b in range(min(2, batches)):
        load_green(b).start()
    for each in (order_load, sort_load, gamma_load):
        each.start()

    tiles = pattern_s.shape[0]
    tile_size = size // tiles
    pattern_load.wait()
    coupling_load.wait()
    lane = lax.broadcasted_iota(jnp.int32, (tile_size, size), 1)
    for i in range(tiles):
        mask = jnp.zeros((tile_size, size), F32)
        for j in range(tiles):
            inside = (lane >= j * tile_size) & (lane < (j + 1) * tile_size)
            mask = jnp.where(inside, pattern_s[i, j].astype(F32), mask)
        at = slice(i * tile_size, (i + 1) * tile_size)
        couple_s[at, :] = (coupling_s[at, :].astype(F32) * mask).astype(BF16)

    @pl.when(cell == 1)
    def _():
        turned_s[...] = jnp.transpose(couple_s[...].astype(F32)).astype(BF16)

    def born(b):
        load_green(b).wait()
        batch = [b * many + i for i in range(many)]

        @pl.when(cell == 0)
        def _():
            couple = couple_s[...]
            green = [green_s[e] for e in batch]
            factor = [dot(g, couple).astype(BF16) for g in green]
            moved = [
                stack(complex_dot(f, g[:rows], g[rows:])).astype(BF16) for f, g in zip(factor, green)
            ]
            for e, f, g, m in zip(batch, factor, green, moved):
                base = g.astype(F32) + stack(complex_dot(m, f[:rows], f[rows:], LAST))
                base_s[e] = base
                send_s[e] = base.astype(BF16)
                mult_s[e] = g
                other_s[e] = g

        @pl.when(cell == 1)
        def _():
            couple = couple_s[...]
            turned = turned_s[...]
            green = [green_s[e] for e in batch]
            flipped = [
                stack((dot(turned, g[:rows], LAST), dot(turned, g[rows:], LAST))).astype(BF16)
                for g in green
            ]
            for e, f in zip(batch, flipped):
                send_s[e] = dot(f, couple).astype(BF16)
                other_s[e] = f
            for e, g in zip(batch, green):
                mult_s[e] = dot(g, couple).astype(BF16)
                base_s[e] = g.astype(F32)

    def lesser(b):
        batch = [b * many + i for i in range(many)]
        mult = [mult_s[e] for e in batch]
        other = [other_s[e] for e in batch]
        moved = [
            stack(complex_dot(m, map_s[e, :rows], map_s[e, rows:])).astype(BF16)
            for e, m in zip(batch, mult)
        ]
        full = [
            (base_s[e] + stack(complex_dot(m, o[:rows], o[rows:]))).astype(BF16)
            for e, m, o in zip(batch, moved, other)
        ]
        weighted = [dot(f, gamma_s[e]).astype(BF16) for e, f in zip(batch, full)]
        found = [
            (
                dot(w[:rows], stack((f[rows:], f[:rows])), LAST)
                + dot(w[rows:], stack((-f[:rows], f[rows:])), LAST)
            ).astype(BF16)
            for w, f in zip(weighted, full)
        ]
        block = 8 * owners
        for q in range(quads):
            at = slice(q * block, (q + 1) * block)
            mixed = sum(dot(pick_s[i, at], found[i]) for i in range(many))
            mixed_s[:, b, :, q * width : (q + 1) * width] = mixed.reshape(owners, 8, width).astype(BF16)

    born(0)
    pl.semaphore_wait(barrier, 1 + len(near))
    share_map(0).start()
    for d in range(1, low):
        say_ready(d)
    for b in range(2, batches):
        load_green(b).start()
    for each in (screened_load, table_load, turn_load, unmix_load):
        each.start()
    if batches > 1:
        born(1)
        share_map(1).start()
    order_load.wait()
    sort_load.wait()
    ids = lax.broadcasted_iota(jnp.int32, (size, size), 0)
    place = jnp.where(ids == order_s[...], 1.0, 0.0).astype(BF16)
    for i in range(many):
        pick_s[i] = dot(sort_s[i], place, LAST).astype(BF16)
    gamma_load.wait()

    for b in range(batches):
        share_map(b).wait_recv()
        lesser(b)
        if b == 0:
            for d in range(low):
                first_away(d)
            keep(0).start()
        if b + 2 < batches:
            born(b + 2)
            share_map(b + 2).start()
    for part in range(1, parts):
        for_peers(lambda k: away(part, k).start())
        keep(part).start()
    turn_load.wait()
    place_s[...] = dot(place, turn_s[...]).astype(BF16)
    table_load.wait()
    screened_load.wait()
    unmix_load.wait()
    table = table_s[...]
    pieces = width // 128
    for r in range(share):
        values = jnp.concatenate(
            [
                screened_s[pl.ds(r * pieces + c, points, stride=share * pieces), :]
                for c in range(pieces)
            ],
            axis=1,
        )
        spectrum_s[:, r * width : (r + 1) * width] = transform(table, values, times_i(values)) * scale

    half = width // 2
    row_ids = lax.broadcasted_iota(jnp.int32, (points, points * pack), 0)
    column_ids = lax.broadcasted_iota(jnp.int32, (points, points * pack), 1)
    for q in range(quads):
        for part in range(parts):
            if q == (early if part == 2 else 0):
                all_away(part, owners, away_landed).wait()
        packed = got_s[:, :, :, q * width : (q + 1) * width].astype(F32)
        packed = packed.reshape(points * pack, width).astype(BF16)
        for r in range(pack):
            if pack == 1:
                values = packed.astype(F32)
            else:
                chosen = jnp.where(column_ids == row_ids * pack + r, 1.0, 0.0).astype(BF16)
                values = dot(chosen, packed)
            at = slice((q * pack + r) * width, (q * pack + r + 1) * width)
            kernel = spectrum_s[:, at]
            spectrum = transform(table, values, times_i(values))
            kernel_re = jnp.concatenate([kernel[:, :half], kernel[:, :half]], axis=1)
            kernel_im = jnp.concatenate([kernel[:, half:], kernel[:, half:]], axis=1)
            product = spectrum * kernel_re + times_i(spectrum) * kernel_im
            found = transform(table, times_i(product), product)
            sigma_s[:, :, at] = found.reshape(owners, here, width).astype(BF16)
        for_peers(lambda k: back(q, k).start())
        keep_back(q).start()

    unmix = unmix_s[...]
    for q in range(quads):
        all_back(q, owners, back_landed).wait()
        for r in range(q * pack, (q + 1) * pack):
            values = back_s[:, :, r * width : (r + 1) * width].astype(F32)
            values = values.reshape(points, width).astype(BF16)
            slots_s[r] = dot(unmix, values).astype(BF16)
    for b in range(batches):
        share_map(b).wait_send()
    for part in range(parts):
        all_away(part, owners - 1, away_sent).wait()
    for q in range(quads):
        all_back(q, owners - 1, back_sent).wait()


def restore_kernel(slots_ref, place_ref, out_ref, result_s, out_sem):
    here, size, width = result_s.shape
    share, points, _ = slots_ref.shape
    owners = points // here
    place = place_ref[...]
    for e in range(here):
        at = slice(e * owners, (e + 1) * owners)
        ordered = jnp.concatenate([slots_ref[r, at, :] for r in range(share)], axis=0)
        result_s[e] = dot(place, ordered)
        out = pltpu.make_async_copy(result_s.at[e], out_ref.at[e], out_sem.at[0])
        out.start()
    pltpu.make_async_copy(result_s, out_ref, out_sem.at[0]).wait()


def on_device(owners, green0, coupling, pattern, broaden, screened, order):
    here = green0.shape[0]
    size = green0.shape[-1]
    points = screened.shape[0]
    share = size // owners
    width = 2 * size
    flat = share * width
    pack = max(p for p in (1, 2, 4) if share % p == 0 and here % (8 // p) == 0)
    quads = share // pack
    many = 8 // pack
    batches = here // many
    early = max(quads - 1, 1)
    green = green0.reshape(here, 2 * size, size)
    gamma = broaden.reshape(here, size, size)

    ticks = np.arange(points)
    angles = (ticks[:, None] * ticks[None, :] % points) * (2.0 * math.pi / points)
    exact = np.concatenate([np.cos(angles), -np.sin(angles)], axis=1)
    high = exact.astype(BF16)
    low = (exact - high.astype(np.float64)).astype(BF16)
    table = jnp.asarray(np.concatenate([high, low], axis=0))
    where = np.arange(points)
    source = (where % owners) * here + where // owners
    unmix = jnp.asarray((source[:, None] == where[None, :]).astype(np.float32).astype(BF16))
    slot = np.arange(size)
    turn = ((slot % owners) * share + slot // owners)[None, :] == slot[:, None]
    turn = jnp.asarray(turn.astype(np.float32).astype(BF16))
    q, o, i, r = np.meshgrid(
        np.arange(quads), np.arange(owners), np.arange(many), np.arange(pack), indexing="ij"
    )
    wanted = (o * share + q * pack + r).reshape(-1)
    owner_of = i.reshape(-1)
    sort = (wanted[None, :, None] == slot[None, None, :]) & (
        owner_of[None, :, None] == np.arange(many)[:, None, None]
    )
    sort = jnp.asarray(sort.astype(np.float32).astype(BF16))

    anywhere = pl.BlockSpec(memory_space=pltpu.HBM)
    dma = pltpu.SemaphoreType.DMA
    cell = (here, 2 * size, size)
    packed = (owners, batches, 8, quads * width)
    vmem = pl.BlockSpec(memory_space=pltpu.VMEM)
    slots, place = pl.pallas_call(
        functools.partial(fused_kernel, owners, pack, 1.0 / (points * math.sqrt(points))),
        in_specs=[anywhere] * 10,
        out_specs=[vmem, vmem],
        out_shape=[
            jax.ShapeDtypeStruct((share, points, width), BF16),
            jax.ShapeDtypeStruct((size, size), BF16),
        ],
        scratch_shapes=[
            pltpu.SMEM(pattern.shape[1:], jnp.int32),
            pltpu.VMEM((size, size), BF16),
            pltpu.VMEM((size, size), BF16),
            pltpu.VMEM((size, size), BF16),
            pltpu.VMEM(cell, BF16),
            pltpu.VMEM((here, size, size), BF16),
            pltpu.VMEM((1, size), jnp.int32),
            pltpu.VMEM(sort.shape, BF16),
            pltpu.VMEM(turn.shape, BF16),
            pltpu.VMEM(table.shape, BF16),
            pltpu.VMEM(unmix.shape, BF16),
            pltpu.VMEM((points * flat // 128, 128), F32),
            pltpu.VMEM(cell, BF16),
            pltpu.VMEM(cell, BF16),
            pltpu.VMEM(cell, F32),
            pltpu.VMEM(cell, BF16),
            pltpu.VMEM(cell, BF16),
            pltpu.VMEM(sort.shape, BF16),
            pltpu.VMEM(packed, BF16),
            pltpu.VMEM(packed, BF16),
            pltpu.VMEM((points, flat), F32),
            pltpu.VMEM((owners, here, flat), BF16),
            pltpu.VMEM((owners, here, flat), BF16),
            dma((9,)),
            dma((batches,)),
            dma((batches,)),
            dma((batches,)),
            dma((3,)),
            dma((3,)),
            dma((quads,)),
            dma((quads,)),
            pltpu.SemaphoreType.REGULAR((1 << (owners.bit_length() - 1) // 2,)),
        ],
        compiler_params=pltpu.CompilerParams(
            collective_id=0, has_side_effects=True, vmem_limit_bytes=44 << 20
        ),
        name="fused",
    )(*(pltpu.with_memory_space_constraint(value, pltpu.HBM) for value in (
        pattern[0],
        coupling[0],
        green,
        gamma,
        order.reshape(1, size),
        sort,
        turn,
        table,
        unmix,
        screened.reshape(points * flat // 128, 128),
    )))
    result = pl.pallas_call(
        restore_kernel,
        in_specs=[vmem, vmem],
        out_specs=anywhere,
        out_shape=jax.ShapeDtypeStruct((here, size, width), F32),
        scratch_shapes=[pltpu.VMEM((here, size, width), F32), dma((1,))],
        compiler_params=pltpu.CompilerParams(vmem_limit_bytes=16 << 20),
        name="restore",
    )(slots, place)
    return result[:, None]


def solution(mesh):
    return jax.shard_map(
        functools.partial(on_device, mesh.shape["energy"]),
        mesh=mesh,
        in_specs=(
            P("energy", "space", None, None, None),
            P("space", None, None),
            P("space", None, None),
            P("energy", "space", None, None),
            P(None, "space", "energy", None),
            P(),
        ),
        out_specs=P("energy", "space", None, None),
        check_vma=False,
    )
```

```python
import functools
import math

import jax
import jax.numpy as jnp
import numpy as np
from jax import lax
from jax.experimental import pallas as pl
from jax.experimental.pallas import tpu as pltpu
from jax.sharding import PartitionSpec as P

F32 = jnp.float32
BF16 = jnp.bfloat16
PLAIN = ((1,), (0,))
LAST = ((1,), (1,))
FIRST = ((0,), (0,))


def dot(a, b, dims=PLAIN):
    return lax.dot_general(a, b, (dims, ((), ())), preferred_element_type=F32)


def complex_dot(left, right_re, right_im, dims=PLAIN):
    rows = left.shape[0] // 2
    with_re = dot(left, right_re, dims)
    with_im = dot(left, right_im, dims)
    return (with_re[:rows] - with_im[rows:], with_im[:rows] + with_re[rows:])


def stack(pair):
    return jnp.concatenate(pair, axis=0)


def times_i(values):
    half = values.shape[1] // 2
    return jnp.concatenate([-values[:, half:], values[:, :half]], axis=1)


def transform(table, upper, lower):
    both = dot(table, jnp.concatenate([upper, lower], axis=0).astype(BF16))
    points = upper.shape[0]
    return both[:points] + both[points:]


def fused_kernel(
    owners,
    pack,
    scale,
    pattern_ref,
    coupling_ref,
    green_ref,
    gamma_ref,
    order_ref,
    sort_ref,
    turn_ref,
    table_ref,
    unmix_ref,
    screened_ref,
    slots_s,
    place_s,
    pattern_s,
    coupling_s,
    couple_s,
    turned_s,
    green_s,
    gamma_s,
    order_s,
    sort_s,
    turn_s,
    table_s,
    unmix_s,
    screened_s,
    mult_s,
    other_s,
    base_s,
    send_s,
    map_s,
    pick_s,
    mixed_s,
    got_s,
    spectrum_s,
    sigma_s,
    back_s,
    load_sem,
    green_sem,
    map_sent,
    map_landed,
    away_sent,
    away_landed,
    back_sent,
    back_landed,
    ready_sem,
):
    me = lax.axis_index("energy")
    cell = lax.axis_index("space")
    here, both, size = green_s.shape
    rows = both // 2
    width = 2 * size
    share = size // owners
    quads = share // pack
    many = 8 // pack
    batches = here // many
    points = owners * here
    early = max(quads - 1, 1)
    parts = 1 if batches == 1 else 2 if quads == 1 else 3

    def load(n, source, target):
        return pltpu.make_async_copy(source, target, load_sem.at[n])

    def load_green(b):
        at = pl.ds(b * many, many)
        return pltpu.make_async_copy(green_ref.at[at], green_s.at[at], green_sem.at[b])

    loads = [
        load(n, source, target)
        for n, (source, target) in enumerate(
            (
                (pattern_ref, pattern_s),
                (coupling_ref, coupling_s),
                (order_ref, order_s),
                (sort_ref, sort_s),
                (gamma_ref, gamma_s),
                (table_ref, table_s),
                (screened_ref, screened_s),
                (turn_ref, turn_s),
                (unmix_ref, unmix_s),
            )
        )
    ]
    pattern_load, coupling_load, order_load, sort_load, gamma_load, table_load, screened_load, turn_load, unmix_load = loads

    doubling = owners & (owners - 1) == 0
    low = 1 << (owners.bit_length() - 1) // 2 if doubling else 1

    def peer_of(k):
        return lax.rem(me + k, owners)

    def partner_of(k):
        return jnp.bitwise_xor(me, k) if doubling else peer_of(k)

    def remote(source, target, sent, landed, device):
        return pltpu.make_async_remote_copy(
            src_ref=source,
            dst_ref=target,
            send_sem=sent,
            recv_sem=landed,
            device_id=device,
            device_id_type=pl.DeviceIdType.MESH,
        )

    def share_map(b):
        at = pl.ds(b * many, many)
        return remote(send_s.at[at], map_s.at[at], map_sent.at[0], map_landed.at[b], {"space": 1 - cell})

    def piece(part):
        if part == 0:
            return pl.ds(0, 1), pl.ds(0, quads * width)
        if part == 1:
            return pl.ds(1, batches - 1), pl.ds(0, early * width)
        return pl.ds(1, batches - 1), pl.ds(early * width, (quads - early) * width)

    def away(part, k):
        peer = peer_of(k) if part else partner_of(k)
        at, columns = piece(part)
        return remote(
            mixed_s.at[peer, at, :, columns],
            got_s.at[me, at, :, columns],
            away_sent.at[0],
            away_landed.at[part],
            {"energy": peer},
        )

    def back(q, k):
        peer = peer_of(k)
        columns = pl.ds(q * pack * width, pack * width)
        return remote(
            sigma_s.at[peer, :, columns],
            back_s.at[me, :, columns],
            back_sent.at[0],
            back_landed.at[q],
            {"energy": peer},
        )

    def keep(part):
        at, columns = piece(part)
        return pltpu.make_async_copy(
            mixed_s.at[me, at, :, columns], got_s.at[me, at, :, columns], away_landed.at[part]
        )

    def keep_back(q):
        columns = pl.ds(q * pack * width, pack * width)
        return pltpu.make_async_copy(
            sigma_s.at[me, :, columns], back_s.at[me, :, columns], back_landed.at[q]
        )

    def all_away(part):
        at, columns = piece(part)
        return pltpu.make_async_copy(
            mixed_s.at[:, at, :, columns], got_s.at[:, at, :, columns], away_landed.at[part]
        )

    def all_back(q):
        columns = pl.ds(q * pack * width, pack * width)
        return pltpu.make_async_copy(
            sigma_s.at[:, :, columns], back_s.at[:, :, columns], back_landed.at[q]
        )

    def for_peers(action):
        lax.fori_loop(1, owners, lambda k, c: (action(k), c)[1], 0)

    barrier = pltpu.get_barrier_semaphore()
    near = list(range(1, low)) + list(range(low, owners, low))

    def greet(device):
        pl.semaphore_signal(barrier, inc=1, device_id=device, device_id_type=pl.DeviceIdType.MESH)

    def say_ready(d):
        pl.semaphore_signal(
            ready_sem.at[d],
            inc=1,
            device_id={"energy": partner_of(d)},
            device_id_type=pl.DeviceIdType.MESH,
        )

    def first_away(d):
        if d:
            pl.semaphore_wait(ready_sem.at[d], 1)
        lax.fori_loop(
            0 if d else 1, owners // low, lambda j, c: (away(0, d + low * j).start(), c)[1], 0
        )

    greet({"space": 1 - cell})
    for distance in near:
        greet({"energy": partner_of(distance)})
    pattern_load.start()
    coupling_load.start()
    for b in range(min(2, batches)):
        load_green(b).start()
    for each in (order_load, sort_load, gamma_load):
        each.start()

    tiles = pattern_s.shape[0]
    tile_size = size // tiles
    pattern_load.wait()
    coupling_load.wait()
    lane = lax.broadcasted_iota(jnp.int32, (tile_size, size), 1)
    for i in range(tiles):
        mask = jnp.zeros((tile_size, size), F32)
        for j in range(tiles):
            inside = (lane >= j * tile_size) & (lane < (j + 1) * tile_size)
            mask = jnp.where(inside, pattern_s[i, j].astype(F32), mask)
        at = slice(i * tile_size, (i + 1) * tile_size)
        couple_s[at, :] = (coupling_s[at, :].astype(F32) * mask).astype(BF16)

    @pl.when(cell == 1)
    def _():
        turned_s[...] = jnp.transpose(couple_s[...].astype(F32)).astype(BF16)

    def born(b):
        load_green(b).wait()
        batch = [b * many + i for i in range(many)]

        @pl.when(cell == 0)
        def _():
            couple = couple_s[...]
            green = [green_s[e] for e in batch]
            factor = [dot(g, couple).astype(BF16) for g in green]
            moved = [
                stack(complex_dot(f, g[:rows], g[rows:])).astype(BF16) for f, g in zip(factor, green)
            ]
            for e, f, g, m in zip(batch, factor, green, moved):
                base = g.astype(F32) + stack(complex_dot(m, f[:rows], f[rows:], LAST))
                base_s[e] = base
                send_s[e] = base.astype(BF16)
                mult_s[e] = g
                other_s[e] = g

        @pl.when(cell == 1)
        def _():
            couple = couple_s[...]
            turned = turned_s[...]
            green = [green_s[e] for e in batch]
            flipped = [
                stack((dot(turned, g[:rows], LAST), dot(turned, g[rows:], LAST))).astype(BF16)
                for g in green
            ]
            for e, f in zip(batch, flipped):
                send_s[e] = dot(f, couple).astype(BF16)
                other_s[e] = f

    def rest(b):
        batch = [b * many + i for i in range(many)]

        @pl.when(cell == 1)
        def _():
            couple = couple_s[...]
            for e in batch:
                green = green_s[e]
                mult_s[e] = dot(green, couple).astype(BF16)
                base_s[e] = green.astype(F32)

    def lesser(b):
        batch = [b * many + i for i in range(many)]
        mult = [mult_s[e] for e in batch]
        other = [other_s[e] for e in batch]
        moved = [
            stack(complex_dot(m, map_s[e, :rows], map_s[e, rows:])).astype(BF16)
            for e, m in zip(batch, mult)
        ]
        full = [
            (base_s[e] + stack(complex_dot(m, o[:rows], o[rows:]))).astype(BF16)
            for e, m, o in zip(batch, moved, other)
        ]
        weighted = [dot(f, gamma_s[e]).astype(BF16) for e, f in zip(batch, full)]
        found = [
            (
                dot(w[:rows], stack((f[rows:], f[:rows])), LAST)
                + dot(w[rows:], stack((-f[:rows], f[rows:])), LAST)
            ).astype(BF16)
            for w, f in zip(weighted, full)
        ]
        block = 8 * owners
        for q in range(quads):
            at = slice(q * block, (q + 1) * block)
            mixed = sum(dot(pick_s[i, at], found[i]) for i in range(many))
            mixed_s[:, b, :, q * width : (q + 1) * width] = mixed.reshape(owners, 8, width).astype(BF16)

    born(0)
    pl.semaphore_wait(barrier, 1 + len(near))
    share_map(0).start()
    for d in range(1, low):
        say_ready(d)
    rest(0)
    for b in range(2, batches):
        load_green(b).start()
    for each in (screened_load, table_load, turn_load, unmix_load):
        each.start()
    if batches > 1:
        born(1)
        share_map(1).start()
        rest(1)
    order_load.wait()
    sort_load.wait()
    ids = lax.broadcasted_iota(jnp.int32, (size, size), 0)
    place = jnp.where(ids == order_s[...], 1.0, 0.0).astype(BF16)
    for i in range(many):
        pick_s[i] = dot(sort_s[i], place, LAST).astype(BF16)
    gamma_load.wait()

    for b in range(batches):
        share_map(b).wait_recv()
        lesser(b)
        if b == 0:
            for d in range(low):
                first_away(d)
            keep(0).start()
        if b + 2 < batches:
            born(b + 2)
            share_map(b + 2).start()
            rest(b + 2)
    for part in range(1, parts):
        for_peers(lambda k: away(part, k).start())
        keep(part).start()
    turn_load.wait()
    place_s[...] = dot(place, turn_s[...]).astype(BF16)
    table_load.wait()
    screened_load.wait()
    unmix_load.wait()
    table = table_s[...]
    pieces = width // 128
    for r in range(share):
        values = jnp.concatenate(
            [
                screened_s[pl.ds(r * pieces + c, points, stride=share * pieces), :]
                for c in range(pieces)
            ],
            axis=1,
        )
        spectrum_s[:, r * width : (r + 1) * width] = transform(table, values, times_i(values)) * scale

    half = width // 2
    row_ids = lax.broadcasted_iota(jnp.int32, (points, points * pack), 0)
    column_ids = lax.broadcasted_iota(jnp.int32, (points, points * pack), 1)
    for q in range(quads):
        for part in range(parts):
            if q == (early if part == 2 else 0):
                all_away(part).wait()
        packed = got_s[:, :, :, q * width : (q + 1) * width].astype(F32)
        packed = packed.reshape(points * pack, width).astype(BF16)
        for r in range(pack):
            if pack == 1:
                values = packed.astype(F32)
            else:
                chosen = jnp.where(column_ids == row_ids * pack + r, 1.0, 0.0).astype(BF16)
                values = dot(chosen, packed)
            at = slice((q * pack + r) * width, (q * pack + r + 1) * width)
            kernel = spectrum_s[:, at]
            spectrum = transform(table, values, times_i(values))
            kernel_re = jnp.concatenate([kernel[:, :half], kernel[:, :half]], axis=1)
            kernel_im = jnp.concatenate([kernel[:, half:], kernel[:, half:]], axis=1)
            product = spectrum * kernel_re + times_i(spectrum) * kernel_im
            found = transform(table, times_i(product), product)
            sigma_s[:, :, at] = found.reshape(owners, here, width).astype(BF16)
        for_peers(lambda k: back(q, k).start())
        keep_back(q).start()

    unmix = unmix_s[...]
    for q in range(quads):
        all_back(q).wait()
        for r in range(q * pack, (q + 1) * pack):
            values = back_s[:, :, r * width : (r + 1) * width].astype(F32)
            values = values.reshape(points, width).astype(BF16)
            slots_s[r] = dot(unmix, values).astype(BF16)
    others = pl.ds(0, owners - 1)
    pltpu.make_async_copy(send_s, map_s, map_sent.at[0]).wait()
    pltpu.make_async_copy(mixed_s.at[others], got_s.at[others], away_sent.at[0]).wait()
    pltpu.make_async_copy(sigma_s.at[others], back_s.at[others], back_sent.at[0]).wait()


def restore_kernel(slots_ref, place_ref, out_ref, result_s, out_sem):
    here, size, width = result_s.shape
    share, points, _ = slots_ref.shape
    owners = points // here
    place = place_ref[...]
    for e in range(here):
        at = slice(e * owners, (e + 1) * owners)
        ordered = jnp.concatenate([slots_ref[r, at, :] for r in range(share)], axis=0)
        result_s[e] = dot(place, ordered)
        out = pltpu.make_async_copy(result_s.at[e], out_ref.at[e], out_sem.at[0])
        out.start()
    pltpu.make_async_copy(result_s, out_ref, out_sem.at[0]).wait()


def on_device(owners, green0, coupling, pattern, broaden, screened, order):
    here = green0.shape[0]
    size = green0.shape[-1]
    points = screened.shape[0]
    share = size // owners
    width = 2 * size
    flat = share * width
    pack = max(p for p in (1, 2, 4) if share % p == 0 and here % (8 // p) == 0)
    quads = share // pack
    many = 8 // pack
    batches = here // many
    early = max(quads - 1, 1)
    green = green0.reshape(here, 2 * size, size)
    gamma = broaden.reshape(here, size, size)

    ticks = np.arange(points)
    angles = (ticks[:, None] * ticks[None, :] % points) * (2.0 * math.pi / points)
    exact = np.concatenate([np.cos(angles), -np.sin(angles)], axis=1)
    high = exact.astype(BF16)
    low = (exact - high.astype(np.float64)).astype(BF16)
    table = jnp.asarray(np.concatenate([high, low], axis=0))
    where = np.arange(points)
    source = (where % owners) * here + where // owners
    unmix = jnp.asarray((source[:, None] == where[None, :]).astype(np.float32).astype(BF16))
    slot = np.arange(size)
    turn = ((slot % owners) * share + slot // owners)[None, :] == slot[:, None]
    turn = jnp.asarray(turn.astype(np.float32).astype(BF16))
    q, o, i, r = np.meshgrid(
        np.arange(quads), np.arange(owners), np.arange(many), np.arange(pack), indexing="ij"
    )
    wanted = (o * share + q * pack + r).reshape(-1)
    owner_of = i.reshape(-1)
    sort = (wanted[None, :, None] == slot[None, None, :]) & (
        owner_of[None, :, None] == np.arange(many)[:, None, None]
    )
    sort = jnp.asarray(sort.astype(np.float32).astype(BF16))

    anywhere = pl.BlockSpec(memory_space=pltpu.HBM)
    dma = pltpu.SemaphoreType.DMA
    cell = (here, 2 * size, size)
    packed = (owners, batches, 8, quads * width)
    vmem = pl.BlockSpec(memory_space=pltpu.VMEM)
    slots, place = pl.pallas_call(
        functools.partial(fused_kernel, owners, pack, 1.0 / (points * math.sqrt(points))),
        in_specs=[anywhere] * 10,
        out_specs=[vmem, vmem],
        out_shape=[
            jax.ShapeDtypeStruct((share, points, width), BF16),
            jax.ShapeDtypeStruct((size, size), BF16),
        ],
        scratch_shapes=[
            pltpu.SMEM(pattern.shape[1:], jnp.int32),
            pltpu.VMEM((size, size), BF16),
            pltpu.VMEM((size, size), BF16),
            pltpu.VMEM((size, size), BF16),
            pltpu.VMEM(cell, BF16),
            pltpu.VMEM((here, size, size), BF16),
            pltpu.VMEM((1, size), jnp.int32),
            pltpu.VMEM(sort.shape, BF16),
            pltpu.VMEM(turn.shape, BF16),
            pltpu.VMEM(table.shape, BF16),
            pltpu.VMEM(unmix.shape, BF16),
            pltpu.VMEM((points * flat // 128, 128), F32),
            pltpu.VMEM(cell, BF16),
            pltpu.VMEM(cell, BF16),
            pltpu.VMEM(cell, F32),
            pltpu.VMEM(cell, BF16),
            pltpu.VMEM(cell, BF16),
            pltpu.VMEM(sort.shape, BF16),
            pltpu.VMEM(packed, BF16),
            pltpu.VMEM(packed, BF16),
            pltpu.VMEM((points, flat), F32),
            pltpu.VMEM((owners, here, flat), BF16),
            pltpu.VMEM((owners, here, flat), BF16),
            dma((9,)),
            dma((batches,)),
            dma((1,)),
            dma((batches,)),
            dma((1,)),
            dma((3,)),
            dma((1,)),
            dma((quads,)),
            pltpu.SemaphoreType.REGULAR((1 << (owners.bit_length() - 1) // 2,)),
        ],
        compiler_params=pltpu.CompilerParams(
            collective_id=0, has_side_effects=True, vmem_limit_bytes=44 << 20
        ),
        name="fused",
    )(*(pltpu.with_memory_space_constraint(value, pltpu.HBM) for value in (
        pattern[0],
        coupling[0],
        green,
        gamma,
        order.reshape(1, size),
        sort,
        turn,
        table,
        unmix,
        screened.reshape(points * flat // 128, 128),
    )))
    result = pl.pallas_call(
        restore_kernel,
        in_specs=[vmem, vmem],
        out_specs=anywhere,
        out_shape=jax.ShapeDtypeStruct((here, size, width), F32),
        scratch_shapes=[pltpu.VMEM((here, size, width), F32), dma((1,))],
        compiler_params=pltpu.CompilerParams(vmem_limit_bytes=16 << 20),
        name="restore",
    )(slots, place)
    return result[:, None]


def solution(mesh):
    return jax.shard_map(
        functools.partial(on_device, mesh.shape["energy"]),
        mesh=mesh,
        in_specs=(
            P("energy", "space", None, None, None),
            P("space", None, None),
            P("space", None, None),
            P("energy", "space", None, None),
            P(None, "space", "energy", None),
            P(),
        ),
        out_specs=P("energy", "space", None, None),
        check_vma=False,
    )
```

```python
import functools
import math

import jax
import jax.numpy as jnp
import numpy as np
from jax import lax
from jax.experimental import pallas as pl
from jax.experimental.pallas import tpu as pltpu
from jax.sharding import PartitionSpec as P

F32 = jnp.float32
BF16 = jnp.bfloat16
PLAIN = ((1,), (0,))
LAST = ((1,), (1,))
FIRST = ((0,), (0,))


def dot(a, b, dims=PLAIN):
    return lax.dot_general(a, b, (dims, ((), ())), preferred_element_type=F32)


def complex_dot(left, right_re, right_im, dims=PLAIN):
    rows = left.shape[0] // 2
    with_re = dot(left, right_re, dims)
    with_im = dot(left, right_im, dims)
    return (with_re[:rows] - with_im[rows:], with_im[:rows] + with_re[rows:])


def stack(pair):
    return jnp.concatenate(pair, axis=0)


def times_i(values):
    half = values.shape[1] // 2
    return jnp.concatenate([-values[:, half:], values[:, :half]], axis=1)


def transform(table, upper, lower):
    both = dot(table, jnp.concatenate([upper, lower], axis=0).astype(BF16))
    points = upper.shape[0]
    return both[:points] + both[points:]


def fused_kernel(
    owners,
    pack,
    scale,
    pattern_ref,
    coupling_ref,
    green_ref,
    gamma_ref,
    order_ref,
    sort_ref,
    turn_ref,
    table_ref,
    unmix_ref,
    screened_ref,
    slots_s,
    place_s,
    pattern_s,
    coupling_s,
    couple_s,
    turned_s,
    green_s,
    gamma_s,
    order_s,
    sort_s,
    turn_s,
    table_s,
    unmix_s,
    screened_s,
    mult_s,
    other_s,
    base_s,
    send_s,
    map_s,
    pick_s,
    mixed_s,
    got_s,
    spectrum_s,
    sigma_s,
    back_s,
    load_sem,
    green_sem,
    map_sent,
    map_landed,
    away_sent,
    away_landed,
    back_sent,
    back_landed,
    ready_sem,
):
    me = lax.axis_index("energy")
    cell = lax.axis_index("space")
    here, both, size = green_s.shape
    rows = both // 2
    width = 2 * size
    share = size // owners
    quads = share // pack
    many = 8 // pack
    batches = here // many
    points = owners * here
    early = max(quads - 1, 1)
    parts = 1 if batches == 1 else 2 if quads == 1 else 3

    def load(n, source, target):
        return pltpu.make_async_copy(source, target, load_sem.at[n])

    def load_green(b):
        at = pl.ds(b * many, many)
        return pltpu.make_async_copy(green_ref.at[at], green_s.at[at], green_sem.at[b])

    loads = [
        load(n, source, target)
        for n, (source, target) in enumerate(
            (
                (pattern_ref, pattern_s),
                (coupling_ref, coupling_s),
                (order_ref, order_s),
                (sort_ref, sort_s),
                (gamma_ref, gamma_s),
                (table_ref, table_s),
                (screened_ref, screened_s),
                (turn_ref, turn_s),
                (unmix_ref, unmix_s),
            )
        )
    ]
    pattern_load, coupling_load, order_load, sort_load, gamma_load, table_load, screened_load, turn_load, unmix_load = loads

    doubling = owners & (owners - 1) == 0
    low = 1 << (owners.bit_length() - 1) // 2 if doubling else 1

    def peer_of(k):
        return lax.rem(me + k, owners)

    def partner_of(k):
        return jnp.bitwise_xor(me, k) if doubling else peer_of(k)

    def remote(source, target, sent, landed, device):
        return pltpu.make_async_remote_copy(
            src_ref=source,
            dst_ref=target,
            send_sem=sent,
            recv_sem=landed,
            device_id=device,
            device_id_type=pl.DeviceIdType.MESH,
        )

    def share_map(b):
        at = pl.ds(b * many, many)
        return remote(send_s.at[at], map_s.at[at], map_sent.at[0], map_landed.at[b], {"space": 1 - cell})

    def piece(part):
        if part == 0:
            return pl.ds(0, 1), pl.ds(0, quads * width)
        if part == 1:
            return pl.ds(1, batches - 1), pl.ds(0, early * width)
        return pl.ds(1, batches - 1), pl.ds(early * width, (quads - early) * width)

    def away(part, k):
        peer = peer_of(k) if part else partner_of(k)
        at, columns = piece(part)
        return remote(
            mixed_s.at[peer, at, :, columns],
            got_s.at[me, at, :, columns],
            away_sent.at[0],
            away_landed.at[part],
            {"energy": peer},
        )

    def back_columns(g):
        count = 1 if g == 0 else quads - 1
        return pl.ds(g * pack * width, count * pack * width)

    def back(q, k):
        peer = peer_of(k)
        columns = back_columns(q)
        return remote(
            sigma_s.at[peer, :, columns],
            back_s.at[me, :, columns],
            back_sent.at[0],
            back_landed.at[q],
            {"energy": peer},
        )

    def keep(part):
        at, columns = piece(part)
        return pltpu.make_async_copy(
            mixed_s.at[me, at, :, columns], got_s.at[me, at, :, columns], away_landed.at[part]
        )

    def keep_back(q):
        columns = back_columns(q)
        return pltpu.make_async_copy(
            sigma_s.at[me, :, columns], back_s.at[me, :, columns], back_landed.at[q]
        )

    def all_away(part):
        at, columns = piece(part)
        return pltpu.make_async_copy(
            mixed_s.at[:, at, :, columns], got_s.at[:, at, :, columns], away_landed.at[part]
        )

    def all_back(q):
        columns = back_columns(q)
        return pltpu.make_async_copy(
            sigma_s.at[:, :, columns], back_s.at[:, :, columns], back_landed.at[q]
        )

    def for_peers(action):
        lax.fori_loop(1, owners, lambda k, c: (action(k), c)[1], 0)

    barrier = pltpu.get_barrier_semaphore()
    near = list(range(1, low)) + list(range(low, owners, low))

    def greet(device):
        pl.semaphore_signal(barrier, inc=1, device_id=device, device_id_type=pl.DeviceIdType.MESH)

    def say_ready(d):
        pl.semaphore_signal(
            ready_sem.at[d],
            inc=1,
            device_id={"energy": partner_of(d)},
            device_id_type=pl.DeviceIdType.MESH,
        )

    def first_away(d):
        if d:
            pl.semaphore_wait(ready_sem.at[d], 1)
        lax.fori_loop(
            0 if d else 1, owners // low, lambda j, c: (away(0, d + low * j).start(), c)[1], 0
        )

    greet({"space": 1 - cell})
    for distance in near:
        greet({"energy": partner_of(distance)})
    pattern_load.start()
    coupling_load.start()
    for b in range(min(2, batches)):
        load_green(b).start()
    for each in (order_load, sort_load, gamma_load):
        each.start()

    tiles = pattern_s.shape[0]
    tile_size = size // tiles
    pattern_load.wait()
    coupling_load.wait()
    lane = lax.broadcasted_iota(jnp.int32, (tile_size, size), 1)
    for i in range(tiles):
        mask = jnp.zeros((tile_size, size), F32)
        for j in range(tiles):
            inside = (lane >= j * tile_size) & (lane < (j + 1) * tile_size)
            mask = jnp.where(inside, pattern_s[i, j].astype(F32), mask)
        at = slice(i * tile_size, (i + 1) * tile_size)
        couple_s[at, :] = (coupling_s[at, :].astype(F32) * mask).astype(BF16)

    @pl.when(cell == 1)
    def _():
        turned_s[...] = jnp.transpose(couple_s[...].astype(F32)).astype(BF16)

    def born(b):
        load_green(b).wait()
        batch = [b * many + i for i in range(many)]

        @pl.when(cell == 0)
        def _():
            couple = couple_s[...]
            green = [green_s[e] for e in batch]
            factor = [dot(g, couple).astype(BF16) for g in green]
            moved = [
                stack(complex_dot(f, g[:rows], g[rows:])).astype(BF16) for f, g in zip(factor, green)
            ]
            for e, f, g, m in zip(batch, factor, green, moved):
                base = g.astype(F32) + stack(complex_dot(m, f[:rows], f[rows:], LAST))
                base_s[e] = base
                send_s[e] = base.astype(BF16)
                mult_s[e] = g
                other_s[e] = g

        @pl.when(cell == 1)
        def _():
            couple = couple_s[...]
            turned = turned_s[...]
            green = [green_s[e] for e in batch]
            flipped = [
                stack((dot(turned, g[:rows], LAST), dot(turned, g[rows:], LAST))).astype(BF16)
                for g in green
            ]
            for e, f in zip(batch, flipped):
                send_s[e] = dot(f, couple).astype(BF16)
                other_s[e] = f

    def rest(b):
        batch = [b * many + i for i in range(many)]

        @pl.when(cell == 1)
        def _():
            couple = couple_s[...]
            for e in batch:
                green = green_s[e]
                mult_s[e] = dot(green, couple).astype(BF16)
                base_s[e] = green.astype(F32)

    def lesser(b):
        batch = [b * many + i for i in range(many)]
        mult = [mult_s[e] for e in batch]
        other = [other_s[e] for e in batch]
        moved = [
            stack(complex_dot(m, map_s[e, :rows], map_s[e, rows:])).astype(BF16)
            for e, m in zip(batch, mult)
        ]
        full = [
            (base_s[e] + stack(complex_dot(m, o[:rows], o[rows:]))).astype(BF16)
            for e, m, o in zip(batch, moved, other)
        ]
        weighted = [dot(f, gamma_s[e]).astype(BF16) for e, f in zip(batch, full)]
        found = [
            (
                dot(w[:rows], stack((f[rows:], f[:rows])), LAST)
                + dot(w[rows:], stack((-f[:rows], f[rows:])), LAST)
            ).astype(BF16)
            for w, f in zip(weighted, full)
        ]
        block = 8 * owners
        for q in range(quads):
            at = slice(q * block, (q + 1) * block)
            mixed = sum(dot(pick_s[i, at], found[i]) for i in range(many))
            mixed_s[:, b, :, q * width : (q + 1) * width] = mixed.reshape(owners, 8, width).astype(BF16)

    born(0)
    pl.semaphore_wait(barrier, 1 + len(near))
    share_map(0).start()
    for d in range(1, low):
        say_ready(d)
    rest(0)
    for b in range(2, batches):
        load_green(b).start()
    for each in (screened_load, table_load, turn_load, unmix_load):
        each.start()
    if batches > 1:
        born(1)
        share_map(1).start()
        rest(1)
    order_load.wait()
    sort_load.wait()
    ids = lax.broadcasted_iota(jnp.int32, (size, size), 0)
    place = jnp.where(ids == order_s[...], 1.0, 0.0).astype(BF16)
    for i in range(many):
        pick_s[i] = dot(sort_s[i], place, LAST).astype(BF16)
    gamma_load.wait()

    for b in range(batches):
        share_map(b).wait_recv()
        lesser(b)
        if b == 0:
            for d in range(low):
                first_away(d)
            keep(0).start()
        if b + 2 < batches:
            born(b + 2)
            share_map(b + 2).start()
            rest(b + 2)
    for part in range(1, parts):
        for_peers(lambda k: away(part, k).start())
        keep(part).start()
    turn_load.wait()
    place_s[...] = dot(place, turn_s[...]).astype(BF16)
    table_load.wait()
    screened_load.wait()
    unmix_load.wait()
    table = table_s[...]
    pieces = width // 128
    for r in range(share):
        values = jnp.concatenate(
            [
                screened_s[pl.ds(r * pieces + c, points, stride=share * pieces), :]
                for c in range(pieces)
            ],
            axis=1,
        )
        spectrum_s[:, r * width : (r + 1) * width] = transform(table, values, times_i(values)) * scale

    half = width // 2
    row_ids = lax.broadcasted_iota(jnp.int32, (points, points * pack), 0)
    column_ids = lax.broadcasted_iota(jnp.int32, (points, points * pack), 1)
    for q in range(quads):
        for part in range(parts):
            if q == (early if part == 2 else 0):
                all_away(part).wait()
        packed = got_s[:, :, :, q * width : (q + 1) * width].astype(F32)
        packed = packed.reshape(points * pack, width).astype(BF16)
        for r in range(pack):
            if pack == 1:
                values = packed.astype(F32)
            else:
                chosen = jnp.where(column_ids == row_ids * pack + r, 1.0, 0.0).astype(BF16)
                values = dot(chosen, packed)
            at = slice((q * pack + r) * width, (q * pack + r + 1) * width)
            kernel = spectrum_s[:, at]
            spectrum = transform(table, values, times_i(values))
            kernel_re = jnp.concatenate([kernel[:, :half], kernel[:, :half]], axis=1)
            kernel_im = jnp.concatenate([kernel[:, half:], kernel[:, half:]], axis=1)
            product = spectrum * kernel_re + times_i(spectrum) * kernel_im
            found = transform(table, times_i(product), product)
            sigma_s[:, :, at] = found.reshape(owners, here, width).astype(BF16)
        if q in (0, quads - 1):
            group = min(q, 1)
            for_peers(lambda k: back(group, k).start())
            keep_back(group).start()

    unmix = unmix_s[...]
    for q in range(quads):
        if q < 2:
            all_back(q).wait()
        for r in range(q * pack, (q + 1) * pack):
            values = back_s[:, :, r * width : (r + 1) * width].astype(F32)
            values = values.reshape(points, width).astype(BF16)
            slots_s[r] = dot(unmix, values).astype(BF16)
    others = pl.ds(0, owners - 1)
    pltpu.make_async_copy(send_s, map_s, map_sent.at[0]).wait()
    pltpu.make_async_copy(mixed_s.at[others], got_s.at[others], away_sent.at[0]).wait()
    pltpu.make_async_copy(sigma_s.at[others], back_s.at[others], back_sent.at[0]).wait()


def restore_kernel(slots_ref, place_ref, out_ref, result_s, out_sem):
    here, size, width = result_s.shape
    share, points, _ = slots_ref.shape
    owners = points // here
    place = place_ref[...]
    for e in range(here):
        at = slice(e * owners, (e + 1) * owners)
        ordered = jnp.concatenate([slots_ref[r, at, :] for r in range(share)], axis=0)
        result_s[e] = dot(place, ordered)
        out = pltpu.make_async_copy(result_s.at[e], out_ref.at[e], out_sem.at[0])
        out.start()
    pltpu.make_async_copy(result_s, out_ref, out_sem.at[0]).wait()


def on_device(owners, green0, coupling, pattern, broaden, screened, order):
    here = green0.shape[0]
    size = green0.shape[-1]
    points = screened.shape[0]
    share = size // owners
    width = 2 * size
    flat = share * width
    pack = max(p for p in (1, 2, 4) if share % p == 0 and here % (8 // p) == 0)
    quads = share // pack
    many = 8 // pack
    batches = here // many
    early = max(quads - 1, 1)
    green = green0.reshape(here, 2 * size, size)
    gamma = broaden.reshape(here, size, size)

    ticks = np.arange(points)
    angles = (ticks[:, None] * ticks[None, :] % points) * (2.0 * math.pi / points)
    exact = np.concatenate([np.cos(angles), -np.sin(angles)], axis=1)
    high = exact.astype(BF16)
    low = (exact - high.astype(np.float64)).astype(BF16)
    table = jnp.asarray(np.concatenate([high, low], axis=0))
    where = np.arange(points)
    source = (where % owners) * here + where // owners
    unmix = jnp.asarray((source[:, None] == where[None, :]).astype(np.float32).astype(BF16))
    slot = np.arange(size)
    turn = ((slot % owners) * share + slot // owners)[None, :] == slot[:, None]
    turn = jnp.asarray(turn.astype(np.float32).astype(BF16))
    q, o, i, r = np.meshgrid(
        np.arange(quads), np.arange(owners), np.arange(many), np.arange(pack), indexing="ij"
    )
    wanted = (o * share + q * pack + r).reshape(-1)
    owner_of = i.reshape(-1)
    sort = (wanted[None, :, None] == slot[None, None, :]) & (
        owner_of[None, :, None] == np.arange(many)[:, None, None]
    )
    sort = jnp.asarray(sort.astype(np.float32).astype(BF16))

    anywhere = pl.BlockSpec(memory_space=pltpu.HBM)
    dma = pltpu.SemaphoreType.DMA
    cell = (here, 2 * size, size)
    packed = (owners, batches, 8, quads * width)
    vmem = pl.BlockSpec(memory_space=pltpu.VMEM)
    slots, place = pl.pallas_call(
        functools.partial(fused_kernel, owners, pack, 1.0 / (points * math.sqrt(points))),
        in_specs=[anywhere] * 10,
        out_specs=[vmem, vmem],
        out_shape=[
            jax.ShapeDtypeStruct((share, points, width), BF16),
            jax.ShapeDtypeStruct((size, size), BF16),
        ],
        scratch_shapes=[
            pltpu.SMEM(pattern.shape[1:], jnp.int32),
            pltpu.VMEM((size, size), BF16),
            pltpu.VMEM((size, size), BF16),
            pltpu.VMEM((size, size), BF16),
            pltpu.VMEM(cell, BF16),
            pltpu.VMEM((here, size, size), BF16),
            pltpu.VMEM((1, size), jnp.int32),
            pltpu.VMEM(sort.shape, BF16),
            pltpu.VMEM(turn.shape, BF16),
            pltpu.VMEM(table.shape, BF16),
            pltpu.VMEM(unmix.shape, BF16),
            pltpu.VMEM((points * flat // 128, 128), F32),
            pltpu.VMEM(cell, BF16),
            pltpu.VMEM(cell, BF16),
            pltpu.VMEM(cell, F32),
            pltpu.VMEM(cell, BF16),
            pltpu.VMEM(cell, BF16),
            pltpu.VMEM(sort.shape, BF16),
            pltpu.VMEM(packed, BF16),
            pltpu.VMEM(packed, BF16),
            pltpu.VMEM((points, flat), F32),
            pltpu.VMEM((owners, here, flat), BF16),
            pltpu.VMEM((owners, here, flat), BF16),
            dma((9,)),
            dma((batches,)),
            dma((1,)),
            dma((batches,)),
            dma((1,)),
            dma((3,)),
            dma((1,)),
            dma((quads,)),
            pltpu.SemaphoreType.REGULAR((1 << (owners.bit_length() - 1) // 2,)),
        ],
        compiler_params=pltpu.CompilerParams(
            collective_id=0, has_side_effects=True, vmem_limit_bytes=44 << 20
        ),
        name="fused",
    )(*(pltpu.with_memory_space_constraint(value, pltpu.HBM) for value in (
        pattern[0],
        coupling[0],
        green,
        gamma,
        order.reshape(1, size),
        sort,
        turn,
        table,
        unmix,
        screened.reshape(points * flat // 128, 128),
    )))
    result = pl.pallas_call(
        restore_kernel,
        in_specs=[vmem, vmem],
        out_specs=anywhere,
        out_shape=jax.ShapeDtypeStruct((here, size, width), F32),
        scratch_shapes=[pltpu.VMEM((here, size, width), F32), dma((1,))],
        compiler_params=pltpu.CompilerParams(vmem_limit_bytes=16 << 20),
        name="restore",
    )(slots, place)
    return result[:, None]


def solution(mesh):
    return jax.shard_map(
        functools.partial(on_device, mesh.shape["energy"]),
        mesh=mesh,
        in_specs=(
            P("energy", "space", None, None, None),
            P("space", None, None),
            P("space", None, None),
            P("energy", "space", None, None),
            P(None, "space", "energy", None),
            P(),
        ),
        out_specs=P("energy", "space", None, None),
        check_vma=False,
    )
```
